32 devices in a mesh: doc: 8 (over z, y), term: 4 (over x, core).
Axes of the slice: x: 2, y: 2, z: 4, core: 2. Of those that a mesh axis runs over, the one named last changes fastest.
Arguments:
- tfidf: bfloat16 [4096, 8192], P('term', 'doc'), may hold values from 50 to 1000
- pattern: int32 [32, 64], P('term', 'doc'), may hold values 0 or 1
- factor_w: bfloat16 [4096, 256], P('term'), may hold values from 0.29882812 to 3
- factor_h: bfloat16 [256, 8192], P(None, 'doc'), may hold values from 0.29882812 to 3
Outputs:
- updated_w: bfloat16 [4096, 256], P('term')
- updated_h: bfloat16 [256, 8192], P(None, 'doc')
The draws below stay inside these ranges and needn't reach their ends.
All inputs are finite; a program needn't handle non-finite values. No bound on the sum of `pattern` on one device may be relied on, other than what follows from the above.
Results may differ from the reference program's by a relative error of at most 0.0004.
The reference program's roundings to bfloat16 on the way count: a program that leaves them out, or rounds other values in their place, can miss the bound.
Values may be sent and summed in bfloat16 or wider, within the bound.
No kernel may reach another device: no remote copies, remote signals or barrier semaphores. Data moves between devices by JAX's collectives and lax.ppermute only.
A program may use at most 64 MiB of HBM per device.

```python
import math
import jax
import jax.numpy as jnp
from jax import lax

K = 256
BLOCK = 128
DOC_DEV = 1024
TERMS = 4096
DOCS = 8192
TERM_BLOCKS = 32
DOC_BLOCKS = 64
N_DOC = 8


def plant(drawn, stream_key, least, high):
    longest = drawn.shape.index(max(drawn.shape))
    spots = []
    for shift in (0, 1):
        where = [jax.random.randint(jax.random.fold_in(stream_key, axis), (), 0, length) for axis, length in enumerate(drawn.shape)]
        where[longest] = (where[longest] + shift) % drawn.shape[longest]
        spots.append(tuple(where))
    return drawn.at[spots[0]].set(least).at[spots[1]].set(high)


def block_scale(rng, extent, split, low, top_value):
    def one(position, blocks):
        steps = jax.random.uniform(jax.random.fold_in(jax.random.fold_in(rng, 6), position), (blocks,), jnp.float32, low / len(split), top_value / len(split))
        return jnp.repeat(jnp.exp(steps), extent[position] // blocks).reshape((-1,) + (1,) * (len(extent) - position - 1))

    level = one(*split[0])
    for cut in split[1:]:
        level = level * one(*cut)
    return level


def setup_inputs(seed: int = 0) -> dict:
    key_of = jax.random.split(jax.random.key(seed), 5)
    tfidf = jnp.clip(jnp.exp(math.log(1000.0) - 2.9957323 * jax.random.uniform(key_of[0], (TERMS, DOCS), jnp.float32) ** block_scale(key_of[0], (TERMS, DOCS), ((0, 4), (1, 8)), -0.2, 0.2)), 50.0, 1000.0).astype(jnp.bfloat16)
    pattern = plant((jax.random.randint(key_of[1], (TERM_BLOCKS, DOC_BLOCKS), 0, 4) < 3).astype(jnp.int32), jax.random.fold_in(key_of[1], 1), 0, 1)
    factor_w = jnp.clip(jnp.exp(math.log(3.0) - 2.306499 * jax.random.uniform(key_of[2], (TERMS, K), jnp.float32) ** block_scale(key_of[2], (TERMS, K), ((0, 4),), -0.2, 0.2)), 0.29882812, 3.0).astype(jnp.bfloat16)
    factor_h = jnp.clip(jnp.exp(math.log(3.0) - 2.306499 * jax.random.uniform(key_of[3], (K, DOCS), jnp.float32) ** block_scale(key_of[3], (K, DOCS), ((1, 8),), -0.2, 0.2)), 0.29882812, 3.0).astype(jnp.bfloat16)
    return dict(tfidf=tfidf, pattern=pattern, factor_w=factor_w, factor_h=factor_h)


def expand(pattern):
    block_rows, block_cols = pattern.shape
    spread = jnp.broadcast_to(pattern[:, None, :, None], (block_rows, BLOCK, block_cols, BLOCK))
    return spread.reshape(block_rows * BLOCK, block_cols * BLOCK)


def reference(tfidf, pattern, factor_w, factor_h):
    gram_w = jnp.dot(factor_w.T, factor_w, preferred_element_type=jnp.float32).astype(jnp.bfloat16)
    per_slab = DOC_DEV // BLOCK

    def visit(totals, slab_index):
        term_topic, gram_sum = totals
        first_col = (slab_index * DOC_DEV).astype(jnp.int32)
        doc_slab = lax.dynamic_slice_in_dim(tfidf, first_col, DOC_DEV, 1)
        slab_mask = expand(lax.dynamic_slice_in_dim(pattern, (slab_index * per_slab).astype(jnp.int32), per_slab, 1))
        doc_slab = doc_slab * slab_mask.astype(doc_slab.dtype)
        old_h = lax.dynamic_slice_in_dim(factor_h, first_col, DOC_DEV, 1)
        numerator = jnp.dot(factor_w.T, doc_slab, preferred_element_type=jnp.float32)
        denominator = jnp.dot(gram_w, old_h, preferred_element_type=jnp.float32)
        new_h = (old_h.astype(jnp.float32) * numerator / denominator).astype(jnp.bfloat16)
        term_topic = term_topic + jnp.dot(doc_slab, new_h.T, preferred_element_type=jnp.float32)
        gram_sum = gram_sum + jnp.dot(new_h, new_h.T, preferred_element_type=jnp.float32)
        return (term_topic, gram_sum), new_h

    start_totals = (jnp.zeros((TERMS, K), jnp.float32), jnp.zeros((K, K), jnp.float32))
    (term_topic, gram_sum), slabs = lax.scan(visit, start_totals, jnp.arange(N_DOC, dtype=jnp.int32))
    updated_h = jnp.transpose(slabs, (1, 0, 2)).reshape(K, DOCS)
    gram_h = gram_sum.astype(jnp.bfloat16)
    denominator = jnp.dot(factor_w, gram_h, preferred_element_type=jnp.float32)
    updated_w = (factor_w.astype(jnp.float32) * term_topic / denominator).astype(jnp.bfloat16)
    return (updated_w, updated_h)
```

```python
import functools

import jax
import jax.numpy as jnp
from jax import lax
from jax.experimental import pallas as pl
from jax.experimental.pallas import tpu as pltpu
from jax.sharding import PartitionSpec as P

BLOCK = 128
F32 = jnp.float32
BF16 = jnp.bfloat16
VMEM = pl.BlockSpec(memory_space=pltpu.VMEM)
SMEM = pl.BlockSpec(memory_space=pltpu.SMEM)


def nt(a, b):
    return lax.dot_general(a, b, (((1,), (1,)), ((), ())), preferred_element_type=F32)


def tn(a, b):
    return lax.dot_general(a, b, (((0,), (0,)), ((), ())), preferred_element_type=F32)


def nn(a, b):
    return lax.dot_general(a, b, (((1,), (0,)), ((), ())), preferred_element_type=F32)


def call(body, out, n_smem, n_vmem, flops=1 << 20, moved=1 << 20, limit=24 << 20):
    return pl.pallas_call(
        body,
        out_shape=out,
        in_specs=[SMEM] * n_smem + [VMEM] * n_vmem,
        out_specs=jax.tree.map(lambda _: VMEM, out),
        compiler_params=pltpu.CompilerParams(vmem_limit_bytes=limit),
        cost_estimate=pl.CostEstimate(flops=flops, bytes_accessed=moved, transcendentals=0),
    )


def like(*shape, dtype=F32):
    return jax.ShapeDtypeStruct(shape, dtype)


def masked_block(pattern, tile_ref, row_block, col_block, rows, cols):
    out = []
    for r in range(rows // BLOCK):
        line = []
        for c in range(cols // BLOCK):
            keep = pattern[row_block + r, col_block + c].astype(F32).astype(BF16)
            part = tile_ref[r * BLOCK : (r + 1) * BLOCK, c * BLOCK : (c + 1) * BLOCK]
            line.append(part * keep)
        out.append(jnp.concatenate(line, axis=1))
    return jnp.concatenate(out, axis=0)


def pack(gram, core):
    k = gram.shape[0]
    h, q = k // 2, k // 4
    e = q // 2
    if core == 0:
        diag, off = gram[:h, :h], gram[:q, h:]
    else:
        diag, off = gram[h:, h:], gram[q:h, h:]
    top = jnp.concatenate([diag[:q], diag[q:]], axis=1)
    low = jnp.concatenate([off[:e], off[e:]], axis=1)
    return jnp.concatenate([top, low], axis=0)


def unpack(one, two):
    k = one.shape[1]
    h, q = k // 2, k // 4
    e = q // 2

    def parts(p):
        diag = jnp.concatenate([p[:q, :h], p[:q, h:]], axis=0)
        off = jnp.concatenate([p[q : q + e, :h], p[q : q + e, h:]], axis=0)
        return diag, off

    diag_one, off_one = parts(one)
    diag_two, off_two = parts(two)
    off = jnp.concatenate([off_one, off_two], axis=0)
    upper = jnp.concatenate([diag_one, off], axis=1)
    lower = jnp.concatenate([off.T, diag_two], axis=1)
    return jnp.concatenate([upper, lower], axis=0)


def pick(core, one, two):
    return jnp.where(core == 0, one, two)


def gram_w_body(place, w, send, keep):
    core = place[0]
    gram = tn(w[...], w[...])
    one, two = pack(gram, 0), pack(gram, 1)
    send[...] = pick(core, two, one)
    keep[...] = pick(core, one, two)


def numer_body(place, pattern, m, w, out, *, cols):
    step = pl.program_id(0)
    rows = m.shape[0]
    tile = masked_block(pattern, m, step * (rows // BLOCK), place[0] * (cols // BLOCK), rows, cols)
    part = tn(w[...], tile)

    @pl.when(step == 0)
    def _():
        out[...] = part

    @pl.when(step > 0)
    def _():
        out[...] += part


def numer(half, pattern, m, w, steps=4):
    terms, docs = m.shape
    k = w.shape[1]
    rows, cols = terms // steps, docs // 2
    return pl.pallas_call(
        functools.partial(numer_body, cols=cols),
        out_shape=like(k, cols),
        grid_spec=pltpu.PrefetchScalarGridSpec(
            num_scalar_prefetch=2,
            grid=(steps,),
            in_specs=[
                pl.BlockSpec((rows, cols), lambda i, place, pat: (i, place[0])),
                pl.BlockSpec((rows, k), lambda i, place, pat: (i, 0)),
            ],
            out_specs=pl.BlockSpec((k, cols), lambda i, place, pat: (0, 0)),
        ),
        compiler_params=pltpu.CompilerParams(vmem_limit_bytes=16 << 20),
        cost_estimate=pl.CostEstimate(
            flops=2 * terms * cols * k, bytes_accessed=2 * terms * cols, transcendentals=0
        ),
    )(half, pattern, m, w)


def add_body(a, b, out):
    out[...] = a[...] + b[...]


def round_add_body(a, b, out):
    out[...] = (a[...] + b[...]).astype(BF16)


def new_h_body(place, mine, other, gram_mine, gram_other, h, out):
    core = place[0]
    cols = mine.shape[1]
    a, b = gram_mine[...], gram_other[...]
    gram = unpack(pick(core, a, b), pick(core, b, a))
    old = h[:, pl.ds(pl.multiple_of(core * cols, cols), cols)]
    total = mine[...] + other[...]
    out[...] = (old.astype(F32) * total / nn(gram, old)).astype(BF16)


def first_w_body(place, pattern, m, h, out):
    rows, cols = m.shape[0], h.shape[1]
    core = place[0]
    step = rows // 2
    for r in range(2):
        view = m.at[pl.ds(r * step, step), pl.ds(pl.multiple_of(core * cols, cols), cols)]
        tile = masked_block(pattern, view, r * (step // BLOCK), core * (cols // BLOCK), step, cols)
        out[r * step : (r + 1) * step, :] = nt(tile, h[...])


def second_w_body(place, pattern, m, part, h, h_own, a_send, a_keep, b_send, b_keep, new_h):
    rows, cols = m.shape[0], h.shape[1]
    core = place[0]
    other = 1 - core
    size = rows // 4

    def piece(start_block):
        start = pl.multiple_of(start_block * size, size)
        view = m.at[pl.ds(start, size), pl.ds(pl.multiple_of(other * cols, cols), cols)]
        tile = masked_block(pattern, view, start_block * (size // BLOCK), other * (cols // BLOCK), size, cols)
        return part[pl.ds(start, size), :] + nt(tile, h[...])

    bit_a, bit_b = place[1], place[2]
    gram = nt(h[...], h[...]) + nt(h_own[...], h_own[...])
    mine = pick(core, pack(gram, 0), pack(gram, 1))
    a_send[:size, :] = piece(1 - bit_a)
    a_send[size:, :] = mine
    b_send[...] = piece(3 - bit_b)
    a_keep[:size, :] = piece(bit_a)
    a_keep[size:, :] = mine
    b_keep[...] = piece(2 + bit_b)
    new_h[:, pl.ds(pl.multiple_of(other * cols, cols), cols)] = h[...]
    new_h[:, pl.ds(pl.multiple_of(core * cols, cols), cols)] = h_own[...]


def halve_body(place, a, ra, b, rb, a_send, a_keep, b_send, b_keep, *, bit_a, bit_b):
    size = b.shape[0] // 2
    tail = a[2 * size :, :] + ra[2 * size :, :]
    for bit, x, rx, send, keep in ((place[bit_a], a, ra, a_send, a_keep), (place[bit_b], b, rb, b_send, b_keep)):
        low = x[:size, :] + rx[:size, :]
        high = x[size : 2 * size, :] + rx[size : 2 * size, :]
        send[:size, :] = jnp.where(bit == 0, high, low)
        keep[:size, :] = jnp.where(bit == 0, low, high)
    a_send[size:, :] = tail
    a_keep[size:, :] = tail


def gram_h_body(a, ra, out, *, size):
    out[...] = (a[size:, :] + ra[size:, :]).astype(BF16)


def new_w_body(place, a, ra, b, rb, gram_mine, gram_other, wa, wb, a_out, b_out):
    core = place[0]
    size = b.shape[0]
    one, two = gram_mine[...], gram_other[...]
    gram = unpack(pick(core, one, two), pick(core, two, one))
    for old_w, mine, other, out in ((wa, a, ra, a_out), (wb, b, rb, b_out)):
        old = old_w[...]
        total = mine[:size, :] + other[:size, :]
        out[...] = (old.astype(F32) * total / nn(old, gram)).astype(BF16)


def swap(x, axis, size, bit):
    return lax.ppermute(x, axis, [(i, i ^ (1 << bit)) for i in range(size)])


def join(bit, mine, other):
    return jnp.concatenate([jnp.where(bit == 0, mine, other), jnp.where(bit == 0, other, mine)], axis=0)


def on_device(m, pattern, w, h, *, n_doc, n_term):
    terms, docs = m.shape
    k = w.shape[1]
    half = docs // 2
    pk = 3 * k // 8
    doc, term = lax.axis_index("doc"), lax.axis_index("term")
    core = term & 1
    bits = n_doc.bit_length() - 1
    order_a = list(range(bits))
    order_b = [1, 0] + list(range(2, bits))
    bit_of = lambda b: (doc >> b) & 1
    place = jnp.stack(
        [core] + [bit_of(b) for b in order_a] + [bit_of(b) for b in order_b]
    ).astype(jnp.int32)
    at_a, at_b = 1, 1 + bits

    def over_term(x, bit):
        return swap(x, "term", n_term, bit)

    def over_doc(x, bit):
        return swap(x, "doc", n_doc, bit)

    g_send, g_keep = call(gram_w_body, (like(pk, k), like(pk, k)), 1, 1)(place, w)
    g_got = over_term(g_send, 0)
    n_send = numer((1 - core)[None], pattern, m, w)
    n_got = over_term(n_send, 0)
    g_sum = call(add_body, like(pk, k), 0, 2)(g_keep, g_got)
    n_keep = numer(core[None], pattern, m, w)
    term_bits = n_term.bit_length() - 1
    for bit in range(1, term_bits - 1):
        g_sum = g_sum + over_term(g_sum, bit)
    g_far = over_term(g_sum, term_bits - 1)
    n_sum = call(add_body, like(k, half), 0, 2)(n_keep, n_got)
    for bit in range(1, term_bits - 1):
        n_sum = n_sum + over_term(n_sum, bit)
    n_far = over_term(n_sum, term_bits - 1)
    g_mine = call(round_add_body, like(pk, k, dtype=BF16), 0, 2)(g_sum, g_far)
    g_other = over_term(g_mine, 0)
    h_own = call(new_h_body, like(k, half, dtype=BF16), 1, 5)(place, n_sum, n_far, g_mine, g_other, h)
    h_other = over_term(h_own, 0)

    flops = terms * docs * k
    part = call(first_w_body, like(terms, k), 2, 2, flops=flops, moved=2 * terms * docs)(place, pattern, m, h_own)
    size = terms // 4
    pick_bits = jnp.stack([core, bit_of(order_a[0]), bit_of(order_b[0])]).astype(jnp.int32)
    a_send, a_keep, b_send, b_keep, new_h = call(
        second_w_body,
        (like(size + pk, k), like(size + pk, k), like(size, k), like(size, k), like(k, docs, dtype=BF16)),
        2,
        4,
        flops=flops,
        moved=2 * terms * docs,
    )(pick_bits, pattern, m, part, h_other, h_own)
    for step in range(bits):
        a_got = over_doc(a_send, order_a[step])
        b_got = over_doc(b_send, order_b[step])
        if step == bits - 1:
            break
        size //= 2
        a_send, a_keep, b_send, b_keep = call(
            functools.partial(halve_body, bit_a=at_a + step + 1, bit_b=at_b + step + 1),
            (like(size + pk, k), like(size + pk, k), like(size, k), like(size, k)),
            1,
            4,
        )(place, a_keep, a_got, b_keep, b_got)
    g_mine = call(functools.partial(gram_h_body, size=size), like(pk, k, dtype=BF16), 0, 2)(a_keep, a_got)
    g_other = over_term(g_mine, 0)
    start_a, start_b = jnp.int32(0), jnp.int32(terms // 2)
    for step in range(bits):
        span = terms // 2 >> (step + 1)
        start_a += bit_of(order_a[step]) * span
        start_b += bit_of(order_b[step]) * span
    old_a = lax.dynamic_slice_in_dim(w, start_a, size, 0)
    old_b = lax.dynamic_slice_in_dim(w, start_b, size, 0)
    w_a, w_b = call(new_w_body, (like(size, k, dtype=BF16), like(size, k, dtype=BF16)), 1, 8)(
        place, a_keep, a_got, b_keep, b_got, g_mine, g_other, old_a, old_b
    )
    for step in reversed(range(bits)):
        w_a = join(bit_of(order_a[step]), w_a, over_doc(w_a, order_a[step]))
        w_b = join(bit_of(order_b[step]), w_b, over_doc(w_b, order_b[step]))
    return jnp.concatenate([w_a, w_b], axis=0), new_h


def solution(mesh):
    sizes = dict(mesh.shape)
    return jax.shard_map(
        functools.partial(on_device, n_doc=sizes["doc"], n_term=sizes["term"]),
        mesh=mesh,
        in_specs=(P("term", "doc"), P("term", "doc"), P("term", None), P(None, "doc")),
        out_specs=(P("term", None), P(None, "doc")),
        check_vma=False,
    )
```

```python
import functools

import jax
import jax.numpy as jnp
from jax import lax
from jax.experimental import pallas as pl
from jax.experimental.pallas import tpu as pltpu
from jax.sharding import PartitionSpec as P


BLOCK = 128
F32 = jnp.float32
BF16 = jnp.bfloat16
VMEM = pl.BlockSpec(memory_space=pltpu.VMEM)
HBM = pl.BlockSpec(memory_space=pltpu.HBM)
PIECES = 4
LIMIT = 50 << 20


def nt(a, b):
    return lax.dot_general(a, b, (((1,), (1,)), ((), ())), preferred_element_type=F32)


def nn(a, b):
    return lax.dot_general(a, b, (((1,), (0,)), ((), ())), preferred_element_type=F32)


def call(body, out, args, hbm=(), scratch=(), flops=1 << 20, moved=1 << 20, limit=24 << 20):
    return pl.pallas_call(
        body,
        out_shape=out,
        in_specs=[HBM if i in hbm else VMEM for i in range(len(args))],
        out_specs=jax.tree.map(lambda _: VMEM, out),
        scratch_shapes=list(scratch),
        compiler_params=pltpu.CompilerParams(vmem_limit_bytes=limit),
        cost_estimate=pl.CostEstimate(flops=flops, bytes_accessed=moved, transcendentals=0),
    )(*args)


def like(*shape, dtype=F32):
    return jax.ShapeDtypeStruct(shape, dtype)


def core_index():
    return lax.axis_index("term") & 1


def doc_bit(bit):
    return (lax.axis_index("doc") >> bit) & 1


def pack(gram, core):
    k = gram.shape[0]
    h, q = k // 2, k // 4
    e = q // 2
    if core == 0:
        diag, off = gram[:h, :h], gram[:q, h:]
    else:
        diag, off = gram[h:, h:], gram[q:h, h:]
    top = jnp.concatenate([diag[:q], diag[q:]], axis=1)
    low = jnp.concatenate([off[:e], off[e:]], axis=1)
    return jnp.concatenate([top, low], axis=0)


def unpack(one, two):
    k = one.shape[1]
    h, q = k // 2, k // 4
    e = q // 2

    def parts(p):
        diag = jnp.concatenate([p[:q, :h], p[:q, h:]], axis=0)
        off = jnp.concatenate([p[q : q + e, :h], p[q : q + e, h:]], axis=0)
        return diag, off

    diag_one, off_one = parts(one)
    diag_two, off_two = parts(two)
    off = jnp.concatenate([off_one, off_two], axis=0)
    upper = jnp.concatenate([diag_one, off], axis=1)
    lower = jnp.concatenate([off.T, diag_two], axis=1)
    return jnp.concatenate([upper, lower], axis=0)


def pick(core, one, two):
    return jnp.where(core == 0, one, two)


def mask_rows(pattern, half, cols):
    blocks = cols // BLOCK
    lane = lax.broadcasted_iota(jnp.int32, (pattern.shape[0], cols), 1) // BLOCK
    mask = jnp.zeros((pattern.shape[0], cols), F32)
    for c in range(blocks):
        column = pick(half, pattern[:, c : c + 1], pattern[:, blocks + c : blocks + c + 1])
        mask = jnp.where(lane == c, column.astype(F32), mask)
    return mask


def masked_piece(tile_ref, mask, piece, rows):
    out = []
    for r in range(rows // BLOCK):
        first = piece * rows + r * BLOCK
        line = mask[first // BLOCK : first // BLOCK + 1, :].astype(BF16)
        out.append(tile_ref[first : first + BLOCK, :] * line)
    return jnp.concatenate(out, axis=0)


def load_body(m, w, wt, send, keep, own, other, w_all, sems):
    core = core_index()
    terms, cols = own.shape
    k = w.shape[1]
    rows = terms // PIECES
    columns = lambda side: pl.ds(pl.multiple_of(side * cols, cols), cols)
    copies = []
    for i in range(PIECES):
        part = pl.ds(i * rows, rows)
        copies.append(pltpu.make_async_copy(w.at[part, :], w_all.at[part, :], sems.at[i]))
    copies.append(pltpu.make_async_copy(m.at[:, columns(1 - core)], other, sems.at[PIECES]))
    copies.append(pltpu.make_async_copy(m.at[:, columns(core)], own, sems.at[PIECES + 1]))
    for copy in copies:
        copy.start()
    gram = jnp.zeros((k, k), F32)
    for i in range(PIECES):
        part = slice(i * rows, (i + 1) * rows)
        copies[i].wait()
        piece = w_all[part, :]
        flipped = piece.T
        wt[:, part] = flipped
        gram += nn(flipped, piece)
    one, two = pack(gram, 0), pack(gram, 1)
    send[...] = pick(core, two, one)
    keep[...] = pick(core, one, two)
    for copy in copies[PIECES:]:
        copy.wait()


def half_h_body(h, out):
    cols = out.shape[1]
    out[...] = h[:, pl.ds(pl.multiple_of(core_index() * cols, cols), cols)]


def numer_body(half, pattern, wt, *refs, other):
    out, masked = refs[-2:]
    side = 1 - core_index() if other else core_index()
    terms, cols = half.shape
    rows = terms // PIECES
    mask = mask_rows(pattern[...], side, cols)
    for i in range(PIECES):
        part = slice(i * rows, (i + 1) * rows)
        tile = masked_piece(half, mask, i, rows)
        masked[part, :] = tile
        product = nn(wt[:, part], tile)
        if i == 0:
            out[...] = product
        else:
            out[...] += product


def add_body(a, b, out):
    out[...] = a[...] + b[...]


def round_add_body(a, b, out):
    out[...] = (a[...] + b[...]).astype(BF16)


def new_h_body(mine, other, gram_mine, gram_other, h, out):
    core = core_index()
    a, b = gram_mine[...], gram_other[...]
    gram = unpack(pick(core, a, b), pick(core, b, a))
    old = h[...]
    total = mine[...] + other[...]
    out[...] = (old.astype(F32) * total / nn(gram, old)).astype(BF16)


def first_w_body(masked, h, out):
    step = masked.shape[0] // 2
    for r in range(2):
        part = slice(r * step, (r + 1) * step)
        out[part, :] = nt(masked[part, :], h[...])


def split_rows(parts, outs, gram, merged):
    size = parts[0][0].shape[0]
    for side in range(2):
        if merged:
            outs[side][:size, :] = parts[0][side]
            outs[side][size : 2 * size, :] = parts[1][side]
            outs[side][2 * size :, :] = gram
        else:
            outs[side][:size, :] = parts[0][side]
            outs[side][size:, :] = gram
            outs[2 + side][...] = parts[1][side]


def second_w_body(masked, part, h, h_own, *outs, bits, merged):
    rows, cols = masked.shape
    core = core_index()
    size = rows // 4
    new_h = outs[-1]

    def piece(start_block):
        start = pl.multiple_of(start_block * size, size)
        return part[pl.ds(start, size), :] + nt(masked[pl.ds(start, size), :], h[...])

    bit_a, bit_b = doc_bit(bits[0]), doc_bit(bits[1])
    gram = nt(h[...], h[...]) + nt(h_own[...], h_own[...])
    mine = pick(core, pack(gram, 0), pack(gram, 1))
    parts = ((piece(1 - bit_a), piece(bit_a)), (piece(3 - bit_b), piece(2 + bit_b)))
    split_rows(parts, outs, mine, merged)
    new_h[:, pl.ds(pl.multiple_of((1 - core) * cols, cols), cols)] = h[...]
    new_h[:, pl.ds(pl.multiple_of(core * cols, cols), cols)] = h_own[...]


def arrived(refs, merged, size):
    if merged:
        total = refs[0][...] + refs[1][...]
        return total[:size], total[size : 2 * size], total[2 * size :]
    a = refs[0][...] + refs[1][...]
    return a[:size], refs[2][...] + refs[3][...], a[size:]


def halve_body(*refs, size, bits, was_merged, merged):
    given = 2 if was_merged else 4
    a, b, gram = arrived(refs[:given], was_merged, size)
    half = size // 2
    parts = []
    for bit, x in ((doc_bit(bits[0]), a), (doc_bit(bits[1]), b)):
        low, high = x[:half], x[half:]
        parts.append((pick(bit, high, low), pick(bit, low, high)))
    split_rows(parts, refs[given:], gram, merged)


def gram_h_body(*refs, size, merged):
    refs[-1][...] = arrived(refs[:-1], merged, size)[2].astype(BF16)


def new_w_body(gram_mine, gram_other, wa, wb, *refs, size, merged):
    core = core_index()
    one, two = gram_mine[...], gram_other[...]
    gram = unpack(pick(core, one, two), pick(core, two, one))
    a, b, _ = arrived(refs[:-1], merged, size)
    out = refs[-1]
    for first, old_ref, total in ((0, wa, a), (size, wb, b)):
        old = old_ref[...]
        out[first : first + size, :] = (old.astype(F32) * total / nn(old, gram)).astype(BF16)


def swap(x, axis, size, bit):
    return lax.ppermute(x, axis, [(i, i ^ (1 << bit)) for i in range(size)])


def join(bit, mine, other):
    return jnp.concatenate([jnp.where(bit == 0, mine, other), jnp.where(bit == 0, other, mine)], axis=0)


def on_device(m, pattern, w, h, *, n_doc, n_term):
    return update(m, pattern, w, h, n_doc, n_term)


def update(m, pattern, w, h, n_doc, n_term):
    terms, docs = m.shape
    k = w.shape[1]
    half = docs // 2
    pk = 3 * k // 8
    bits = n_doc.bit_length() - 1
    term_bits = n_term.bit_length() - 1
    order = [tuple(pair) for pair in zip(range(bits), [1, 0] + list(range(2, bits)))]
    same = [one == two for one, two in order]

    def over_term(x, bit):
        return swap(x, "term", n_term, bit)

    def over_doc(x, bit):
        return swap(x, "doc", n_doc, bit)

    flops = terms * docs * k
    moved = 2 * terms * docs

    side = like(terms, half, dtype=BF16)
    wt, g_send, g_keep, own, other = call(
        load_body,
        (like(k, terms, dtype=BF16), like(pk, k), like(pk, k), side, side),
        (m, w),
        hbm=(0, 1),
        scratch=(pltpu.VMEM((terms, k), BF16), pltpu.SemaphoreType.DMA((PIECES + 2,))),
        limit=LIMIT,
    )
    g_got = over_term(g_send, 0)

    def numer(half_m, is_other, *after):
        body = functools.partial(numer_body, other=is_other)
        return call(body, (like(k, half), side), (half_m, pattern, wt, *after), flops=flops, moved=moved)

    n_send, masked_other = numer(other, True)
    n_got = over_term(n_send, 0)
    g_sum = call(add_body, like(pk, k), (g_keep, g_got))
    for bit in range(1, term_bits - 1):
        g_sum = g_sum + over_term(g_sum, bit)
    g_far = over_term(g_sum, term_bits - 1)
    n_keep, masked_own = numer(own, False, g_sum)
    h_old = call(half_h_body, like(k, half, dtype=BF16), (h,))
    n_sum = call(add_body, like(k, half), (n_keep, n_got))
    for bit in range(1, term_bits - 1):
        n_sum = n_sum + over_term(n_sum, bit)
    n_far = over_term(n_sum, term_bits - 1)
    g_mine = call(round_add_body, like(pk, k, dtype=BF16), (g_sum, g_far))
    g_other = over_term(g_mine, 0)
    h_own = call(new_h_body, like(k, half, dtype=BF16), (n_sum, n_far, g_mine, g_other, h_old))
    h_other = over_term(h_own, 0)

    part = call(first_w_body, like(terms, k), (masked_own, h_own), flops=flops, moved=moved)
    size = terms // 4

    def pieces(rows, merged):
        if merged:
            return (like(2 * rows + pk, k),) * 2
        return (like(rows + pk, k),) * 2 + (like(rows, k),) * 2

    *state, new_h = call(
        functools.partial(second_w_body, bits=order[0], merged=same[0]),
        pieces(size, same[0]) + (like(k, docs, dtype=BF16),),
        (masked_other, part, h_other, h_own),
        flops=flops,
        moved=moved,
    )
    for step in range(bits):
        got = [over_doc(state[2 * i], order[step][i]) for i in range(len(state) // 2)]
        refs = []
        for i, x in enumerate(got):
            refs += [state[2 * i + 1], x]
        if step == bits - 1:
            break
        body = functools.partial(
            halve_body, size=size, bits=order[step + 1], was_merged=same[step], merged=same[step + 1]
        )
        size //= 2
        state = call(body, pieces(size, same[step + 1]), refs)
    merged = same[bits - 1]
    g_mine = call(functools.partial(gram_h_body, size=size, merged=merged), like(pk, k, dtype=BF16), refs)
    g_other = over_term(g_mine, 0)
    old = []
    for stream in range(2):
        start = jnp.int32(stream * (terms // 2))
        for step in range(bits):
            start += doc_bit(order[step][stream]) * (terms // 2 >> (step + 1))
        old.append(lax.dynamic_slice_in_dim(w, start, size, 0))
    both = call(
        functools.partial(new_w_body, size=size, merged=merged),
        like(2 * size, k, dtype=BF16),
        (g_mine, g_other, *old, *refs),
    )
    for step in reversed(range(bits)):
        if same[step]:
            got = over_doc(both, order[step][0])
            w_a, w_b = [
                join(doc_bit(order[step][0]), both[i * size : (i + 1) * size], got[i * size : (i + 1) * size])
                for i in range(2)
            ]
        else:
            w_a, w_b = both[:size], both[size:]
            w_a, w_b = [
                join(doc_bit(bit), x, over_doc(x, bit)) for x, bit in zip((w_a, w_b), order[step])
            ]
        size *= 2
        both = jnp.concatenate([w_a, w_b], axis=0)
    return both, new_h


def solution(mesh):
    sizes = dict(mesh.shape)
    return jax.shard_map(
        functools.partial(on_device, n_doc=sizes["doc"], n_term=sizes["term"]),
        mesh=mesh,
        in_specs=(P("term", "doc"), P("term", "doc"), P("term", None), P(None, "doc")),
        out_specs=(P("term", None), P(None, "doc")),
        check_vma=False,
    )
```

```python
import functools

import jax
import jax.numpy as jnp
from jax import lax
from jax.experimental import pallas as pl
from jax.experimental.pallas import tpu as pltpu
from jax.sharding import PartitionSpec as P


BLOCK = 128
F32 = jnp.float32
BF16 = jnp.bfloat16
VMEM = pl.BlockSpec(memory_space=pltpu.VMEM)
HBM = pl.BlockSpec(memory_space=pltpu.HBM)
PIECES = 4
LIMIT = 50 << 20
TABLE = 16


def nt(a, b):
    return lax.dot_general(a, b, (((1,), (1,)), ((), ())), preferred_element_type=F32)


def nn(a, b):
    return lax.dot_general(a, b, (((1,), (0,)), ((), ())), preferred_element_type=F32)


def call(body, out, args, hbm=(), scratch=(), flops=1 << 20, moved=1 << 20, limit=24 << 20):
    return pl.pallas_call(
        body,
        out_shape=out,
        in_specs=[HBM if i in hbm else VMEM for i in range(len(args))],
        out_specs=jax.tree.map(lambda _: VMEM, out),
        scratch_shapes=list(scratch),
        compiler_params=pltpu.CompilerParams(vmem_limit_bytes=limit),
        cost_estimate=pl.CostEstimate(flops=flops, bytes_accessed=moved, transcendentals=0),
    )(*args)


def like(*shape, dtype=F32):
    return jax.ShapeDtypeStruct(shape, dtype)


LEVELS = 65534
PER_OCTAVE = 512
EMPTY = -32768


def limits(low, high):
    empty = high == EMPTY
    least = jnp.where(empty, 0.0, jnp.exp2(low * (1.0 / PER_OCTAVE)))
    step = jnp.where(empty, 0.0, (jnp.exp2(high * (1.0 / PER_OCTAVE)) - least) * (1.0 / LEVELS))
    return least, step


def encode(x):
    least = jnp.min(x, axis=0, keepdims=True)
    most = jnp.max(x, axis=0, keepdims=True)
    octave = lambda v: jnp.log2(jnp.maximum(v, 1e-18)) * PER_OCTAVE
    empty = most <= 0.0
    low = jnp.where(empty, EMPTY, jnp.floor(octave(least) - 0.5)).astype(F32)
    high = jnp.where(empty, EMPTY, jnp.ceil(octave(most) + 0.5)).astype(F32)
    base, step = limits(low, high)
    scale = jnp.where(empty, 0.0, 1.0 / jnp.where(empty, 1.0, step))
    code = jnp.clip((x - base) * scale + 0.5, 0.0, LEVELS).astype(jnp.int32) - LEVELS // 2
    return code, low, high


def decode(code, low, high):
    base, step = limits(low, high)
    return base + (code.astype(jnp.int32) + LEVELS // 2).astype(F32) * step


def put_codes(ref, first, groups):
    table = []
    for x in groups:
        code, low, high = encode(x)
        ref[first : first + x.shape[0], :] = code.astype(jnp.int16)
        table += [low, high]
        first += x.shape[0]
    return table


def put_table(ref, at, table):
    row = lax.broadcasted_iota(jnp.int32, (TABLE, table[0].shape[1]), 0)
    out = jnp.zeros(row.shape, F32)
    for i, line in enumerate(table):
        out = jnp.where(row == i, line, out)
    ref[at : at + TABLE, :] = out.astype(jnp.int32).astype(jnp.int16)


def get_table(ref, at):
    return ref[at : at + TABLE, :].astype(jnp.int32).astype(F32)


def get_codes(ref, first, rows, group, table, entry):
    out = []
    for i in range(rows // group):
        low, high = table[entry : entry + 1, :], table[entry + 1 : entry + 2, :]
        out.append(decode(ref[first + i * group : first + (i + 1) * group, :], low, high))
        entry += 2
    return jnp.concatenate(out, axis=0)


def put_gram(ref, first, gram):
    high = jnp.ceil(jnp.log2(jnp.max(gram, axis=0, keepdims=True) + 1e-18) * PER_OCTAVE + 0.5)
    unit = float(1 << 30) / jnp.exp2(high * (1.0 / PER_OCTAVE))
    code = (gram * unit).astype(jnp.int32)
    rows = gram.shape[0]
    ref[first : first + rows, :] = (code >> 15).astype(jnp.int16)
    ref[first + rows : first + 2 * rows, :] = (code & 32767).astype(jnp.int16)
    return high


def get_gram(ref, first, rows, high):
    code = (ref[first : first + rows, :].astype(jnp.int32) << 15) + ref[first + rows : first + 2 * rows, :].astype(jnp.int32)
    return code.astype(F32) * (jnp.exp2(high * (1.0 / PER_OCTAVE)) * (1.0 / (1 << 30)))


def core_index():
    return lax.axis_index("term") & 1


def doc_bit(bit):
    return (lax.axis_index("doc") >> bit) & 1


def pack(gram, core):
    k = gram.shape[0]
    h, q = k // 2, k // 4
    e = q // 2
    if core == 0:
        diag, off = gram[:h, :h], gram[:q, h:]
    else:
        diag, off = gram[h:, h:], gram[q:h, h:]
    top = jnp.concatenate([diag[:q], diag[q:]], axis=1)
    low = jnp.concatenate([off[:e], off[e:]], axis=1)
    return jnp.concatenate([top, low], axis=0)


def unpack(one, two):
    k = one.shape[1]
    h, q = k // 2, k // 4
    e = q // 2

    def parts(p):
        diag = jnp.concatenate([p[:q, :h], p[:q, h:]], axis=0)
        off = jnp.concatenate([p[q : q + e, :h], p[q : q + e, h:]], axis=0)
        return diag, off

    diag_one, off_one = parts(one)
    diag_two, off_two = parts(two)
    off = jnp.concatenate([off_one, off_two], axis=0)
    upper = jnp.concatenate([diag_one, off], axis=1)
    lower = jnp.concatenate([off.T, diag_two], axis=1)
    return jnp.concatenate([upper, lower], axis=0)


def pick(core, one, two):
    return jnp.where(core == 0, one, two)


def mask_rows(pattern, half, cols):
    blocks = cols // BLOCK
    lane = lax.broadcasted_iota(jnp.int32, (pattern.shape[0], cols), 1) // BLOCK
    mask = jnp.zeros((pattern.shape[0], cols), F32)
    for c in range(blocks):
        column = pick(half, pattern[:, c : c + 1], pattern[:, blocks + c : blocks + c + 1])
        mask = jnp.where(lane == c, column.astype(F32), mask)
    return mask


def masked_piece(tile_ref, mask, piece, rows):
    out = []
    for r in range(rows // BLOCK):
        first = piece * rows + r * BLOCK
        line = mask[first // BLOCK : first // BLOCK + 1, :].astype(BF16)
        out.append(tile_ref[first : first + BLOCK, :] * line)
    return jnp.concatenate(out, axis=0)


def load_body(m, w, wt, send, keep, own, other, w_all, sems):
    core = core_index()
    terms, cols = own.shape
    k = w.shape[1]
    rows = terms // PIECES
    columns = lambda side: pl.ds(pl.multiple_of(side * cols, cols), cols)
    copies = []
    for i in range(PIECES):
        part = pl.ds(i * rows, rows)
        copies.append(pltpu.make_async_copy(w.at[part, :], w_all.at[part, :], sems.at[i]))
    copies.append(pltpu.make_async_copy(m.at[:, columns(1 - core)], other, sems.at[PIECES]))
    copies.append(pltpu.make_async_copy(m.at[:, columns(core)], own, sems.at[PIECES + 1]))
    for copy in copies:
        copy.start()
    gram = jnp.zeros((k, k), F32)
    for i in range(PIECES):
        part = slice(i * rows, (i + 1) * rows)
        copies[i].wait()
        piece = w_all[part, :]
        flipped = piece.T
        wt[:, part] = flipped
        gram += nn(flipped, piece)
    one, two = pack(gram, 0), pack(gram, 1)
    send[...] = pick(core, two, one)
    keep[...] = pick(core, one, two)
    for copy in copies[PIECES:]:
        copy.wait()


def half_h_body(h, out):
    cols = out.shape[1]
    out[...] = h[:, pl.ds(pl.multiple_of(core_index() * cols, cols), cols)]


def numer_body(half, pattern, wt, *refs, other):
    out, masked = refs[-2:]
    side = 1 - core_index() if other else core_index()
    terms, cols = half.shape
    rows = terms // PIECES
    mask = mask_rows(pattern[...], side, cols)
    for i in range(PIECES):
        part = slice(i * rows, (i + 1) * rows)
        tile = masked_piece(half, mask, i, rows)
        masked[part, :] = tile
        product = nn(wt[:, part], tile)
        if i == 0:
            out[...] = product
        else:
            out[...] += product


def add_body(a, b, out):
    out[...] = a[...] + b[...]


def round_add_body(a, b, out):
    out[...] = (a[...] + b[...]).astype(BF16)


def code_sum_body(a, b, out):
    rows = a.shape[0]
    table = put_codes(out, 0, [a[...] + b[...]])
    put_table(out, rows, table)


def new_h_body(mine, other, gram_mine, gram_other, h, out):
    core = core_index()
    a, b = gram_mine[...], gram_other[...]
    gram = unpack(pick(core, a, b), pick(core, b, a))
    old = h[...]
    rows = h.shape[0]
    total = None
    for ref in (mine, other):
        part = get_codes(ref, 0, rows, rows, get_table(ref, rows), 0)
        total = part if total is None else total + part
    out[...] = (old.astype(F32) * total / nn(gram, old)).astype(BF16)


def first_w_body(masked, h, out):
    step = masked.shape[0] // 2
    for r in range(2):
        part = slice(r * step, (r + 1) * step)
        out[part, :] = nt(masked[part, :], h[...])


def blocks_of(x):
    group = min(BLOCK, x.shape[0])
    return [x[i : i + group] for i in range(0, x.shape[0], group)]


def store_step(sent, gram, outs, merged):
    if merged:
        groups = blocks_of(sent[0]) + blocks_of(sent[1])
        at = 2 * sent[0].shape[0]
    else:
        groups = blocks_of(sent[0])
        at = sent[0].shape[0]
        table = put_codes(outs[1], 0, blocks_of(sent[1]))
        put_table(outs[1], at, table)
    table = put_codes(outs[0], 0, groups)
    table.append(put_gram(outs[0], at + TABLE, gram))
    put_table(outs[0], at, table)


def arrived(sent, got, size, pk, merged):
    at = 2 * size if merged else size
    group = min(BLOCK, size)
    entry = 2 * (at // group)
    table = get_table(got[0], at)
    own_table = get_table(sent[0], at)
    gram = get_gram(sent[0], at + TABLE, pk, own_table[entry : entry + 1, :]) + get_gram(
        got[0], at + TABLE, pk, table[entry : entry + 1, :]
    )
    if merged:
        both = get_codes(got[0], 0, at, group, table, 0)
        return both[:size], both[size:], gram
    a = get_codes(got[0], 0, size, group, table, 0)
    b = get_codes(got[1], 0, size, group, get_table(got[1], size), 0)
    return a, b, gram


def second_w_body(masked, part, h, h_own, *outs, bits):
    rows, cols = masked.shape
    core = core_index()
    size = rows // 4
    keep_a, keep_b, new_h = outs[-3:]

    def piece(start_block):
        start = pl.multiple_of(start_block * size, size)
        return part[pl.ds(start, size), :] + nt(masked[pl.ds(start, size), :], h[...])

    bit_a, bit_b = doc_bit(bits[0]), doc_bit(bits[1])
    gram = nt(h[...], h[...]) + nt(h_own[...], h_own[...])
    mine = pick(core, pack(gram, 0), pack(gram, 1))
    store_step((piece(1 - bit_a), piece(3 - bit_b)), mine, outs, False)
    keep_a[...] = piece(bit_a)
    keep_b[...] = piece(2 + bit_b)
    new_h[:, pl.ds(pl.multiple_of((1 - core) * cols, cols), cols)] = h[...]
    new_h[:, pl.ds(pl.multiple_of(core * cols, cols), cols)] = h_own[...]


def next_step_body(keep_a, keep_b, *refs, size, pk, bits, was_merged, merged, last):
    streams = 1 if was_merged else 2
    sent, got, outs = refs[:streams], refs[streams : 2 * streams], refs[2 * streams :]
    a, b, gram = arrived(sent, got, size, pk, was_merged)
    a, b = keep_a[...] + a, keep_b[...] + b
    if last:
        store_step((a, b), gram, outs, True)
        return
    half = size // 2
    sends = []
    for bit, x, keep in ((doc_bit(bits[0]), a, outs[-2]), (doc_bit(bits[1]), b, outs[-1])):
        low, high = x[:half], x[half:]
        sends.append(pick(bit, high, low))
        keep[...] = pick(bit, low, high)
    store_step(sends, gram, outs, merged)


def gram_h_body(sent, got, out, *, size, pk):
    at, entry = 2 * size, 4 * size // min(BLOCK, size)
    parts = [get_gram(ref, at + TABLE, pk, get_table(ref, at)[entry : entry + 1, :]) for ref in (sent, got)]
    out[...] = (parts[0] + parts[1]).astype(BF16)


def new_w_body(gram_mine, gram_other, wa, wb, sent, got, out, *, size):
    core = core_index()
    one, two = gram_mine[...], gram_other[...]
    gram = unpack(pick(core, one, two), pick(core, two, one))
    group = min(BLOCK, size)
    parts = [get_codes(ref, 0, 2 * size, group, get_table(ref, 2 * size), 0) for ref in (sent, got)]
    total = parts[0] + parts[1]
    for first, old_ref in ((0, wa), (size, wb)):
        old = old_ref[...]
        part = slice(first, first + size)
        out[part, :] = (old.astype(F32) * total[part] / nn(old, gram)).astype(BF16)


def swap(x, axis, size, bit):
    return lax.ppermute(x, axis, [(i, i ^ (1 << bit)) for i in range(size)])


def join(bit, mine, other):
    return jnp.concatenate([jnp.where(bit == 0, mine, other), jnp.where(bit == 0, other, mine)], axis=0)


def on_device(m, pattern, w, h, *, n_doc, n_term):
    return update(m, pattern, w, h, n_doc, n_term)


def update(m, pattern, w, h, n_doc, n_term):
    terms, docs = m.shape
    k = w.shape[1]
    half = docs // 2
    pk = 3 * k // 8
    bits = n_doc.bit_length() - 1
    term_bits = n_term.bit_length() - 1
    order = [tuple(pair) for pair in zip(range(bits), [1, 0] + list(range(2, bits)))]
    same = [one == two for one, two in order]

    def over_term(x, bit):
        return swap(x, "term", n_term, bit)

    def over_doc(x, bit):
        return swap(x, "doc", n_doc, bit)

    flops = terms * docs * k
    moved = 2 * terms * docs

    side = like(terms, half, dtype=BF16)
    wt, g_send, g_keep, own, other = call(
        load_body,
        (like(k, terms, dtype=BF16), like(pk, k), like(pk, k), side, side),
        (m, w),
        hbm=(0, 1),
        scratch=(pltpu.VMEM((terms, k), BF16), pltpu.SemaphoreType.DMA((PIECES + 2,))),
        limit=LIMIT,
    )
    g_got = over_term(g_send, 0)

    def numer(half_m, is_other, *after):
        body = functools.partial(numer_body, other=is_other)
        return call(body, (like(k, half), side), (half_m, pattern, wt, *after), flops=flops, moved=moved)

    n_send, masked_other = numer(other, True)
    n_got = over_term(n_send, 0)
    g_sum = call(add_body, like(pk, k), (g_keep, g_got))
    for bit in range(1, term_bits - 1):
        g_sum = g_sum + over_term(g_sum, bit)
    g_far = over_term(g_sum, term_bits - 1)
    n_keep, masked_own = numer(own, False, g_sum)
    h_old = call(half_h_body, like(k, half, dtype=BF16), (h,))
    for bit in range(1, term_bits - 1):
        n_keep = call(add_body, like(k, half), (n_keep, n_got))
        n_got = over_term(n_keep, bit)
    n_sum = call(code_sum_body, like(k + TABLE, half, dtype=jnp.int16), (n_keep, n_got))
    n_far = over_term(n_sum, term_bits - 1)
    g_mine = call(round_add_body, like(pk, k, dtype=BF16), (g_sum, g_far))
    g_other = over_term(g_mine, 0)
    h_own = call(new_h_body, like(k, half, dtype=BF16), (n_sum, n_far, g_mine, g_other, h_old))
    h_other = over_term(h_own, 0)

    part = call(first_w_body, like(terms, k), (masked_own, h_own), flops=flops, moved=moved)
    size = terms // 4

    def payloads(rows, merged):
        if merged:
            return (like(2 * rows + TABLE + 2 * pk, k, dtype=jnp.int16),)
        return (like(rows + TABLE + 2 * pk, k, dtype=jnp.int16), like(rows + TABLE, k, dtype=jnp.int16))

    *sent, keep_a, keep_b, new_h = call(
        functools.partial(second_w_body, bits=order[0]),
        payloads(size, False) + (like(size, k),) * 2 + (like(k, docs, dtype=BF16),),
        (masked_other, part, h_other, h_own),
        flops=flops,
        moved=moved,
    )
    for step in range(bits):
        got = [over_doc(x, order[step][i]) for i, x in enumerate(sent)]
        if step == bits - 1:
            break
        last = step == bits - 2
        body = functools.partial(
            next_step_body,
            size=size,
            pk=pk,
            bits=order[step + 1],
            was_merged=same[step],
            merged=same[step + 1],
            last=last,
        )
        args = (keep_a, keep_b, *sent, *got)
        if last:
            sent = call(body, payloads(size, True), args)
        else:
            size //= 2
            *sent, keep_a, keep_b = call(body, payloads(size, same[step + 1]) + (like(size, k),) * 2, args)
    ends = (sent[0], got[0])
    g_mine = call(functools.partial(gram_h_body, size=size, pk=pk), like(pk, k, dtype=BF16), ends)
    g_other = over_term(g_mine, 0)
    old = []
    for stream in range(2):
        start = jnp.int32(stream * (terms // 2))
        for step in range(bits - 1):
            start += doc_bit(order[step][stream]) * (terms // 2 >> (step + 1))
        old.append(lax.dynamic_slice_in_dim(w, start, size, 0))
    both = call(
        functools.partial(new_w_body, size=size),
        like(2 * size, k, dtype=BF16),
        (g_mine, g_other, *old, *ends),
    )
    for step in reversed(range(bits - 1)):
        if same[step]:
            got = over_doc(both, order[step][0])
            w_a, w_b = [
                join(doc_bit(order[step][0]), both[i * size : (i + 1) * size], got[i * size : (i + 1) * size])
                for i in range(2)
            ]
        else:
            w_a, w_b = both[:size], both[size:]
            w_a, w_b = [
                join(doc_bit(bit), x, over_doc(x, bit)) for x, bit in zip((w_a, w_b), order[step])
            ]
        size *= 2
        both = jnp.concatenate([w_a, w_b], axis=0)
    return both, new_h


def solution(mesh):
    sizes = dict(mesh.shape)
    return jax.shard_map(
        functools.partial(on_device, n_doc=sizes["doc"], n_term=sizes["term"]),
        mesh=mesh,
        in_specs=(P("term", "doc"), P("term", "doc"), P("term", None), P(None, "doc")),
        out_specs=(P("term", None), P(None, "doc")),
        check_vma=False,
    )
```

```python
import functools

import jax
import jax.numpy as jnp
from jax import lax
from jax.experimental import pallas as pl
from jax.experimental.pallas import tpu as pltpu
from jax.sharding import PartitionSpec as P


BLOCK = 128
F32 = jnp.float32
BF16 = jnp.bfloat16
VMEM = pl.BlockSpec(memory_space=pltpu.VMEM)
HBM = pl.BlockSpec(memory_space=pltpu.HBM)
PIECES = 4
LIMIT = 50 << 20
TABLE = 16


def nt(a, b):
    return lax.dot_general(a, b, (((1,), (1,)), ((), ())), preferred_element_type=F32)


def nn(a, b):
    return lax.dot_general(a, b, (((1,), (0,)), ((), ())), preferred_element_type=F32)


def call(body, out, args, hbm=(), scratch=(), flops=1 << 20, moved=1 << 20, limit=24 << 20):
    return pl.pallas_call(
        body,
        out_shape=out,
        in_specs=[HBM if i in hbm else VMEM for i in range(len(args))],
        out_specs=jax.tree.map(lambda _: VMEM, out),
        scratch_shapes=list(scratch),
        compiler_params=pltpu.CompilerParams(vmem_limit_bytes=limit),
        cost_estimate=pl.CostEstimate(flops=flops, bytes_accessed=moved, transcendentals=0),
    )(*args)


def like(*shape, dtype=F32):
    return jax.ShapeDtypeStruct(shape, dtype)


LEVELS = 65534
PER_OCTAVE = 512
EMPTY = -32768


def limits(low, high):
    empty = high == EMPTY
    least = jnp.where(empty, 0.0, jnp.exp2(low * (1.0 / PER_OCTAVE)))
    step = jnp.where(empty, 0.0, (jnp.exp2(high * (1.0 / PER_OCTAVE)) - least) * (1.0 / LEVELS))
    return least, step


def encode(x):
    least = jnp.min(x, axis=0, keepdims=True)
    most = jnp.max(x, axis=0, keepdims=True)
    octave = lambda v: jnp.log2(jnp.maximum(v, 1e-18)) * PER_OCTAVE
    empty = most <= 0.0
    low = jnp.where(empty, EMPTY, jnp.floor(octave(least) - 0.5)).astype(F32)
    high = jnp.where(empty, EMPTY, jnp.ceil(octave(most) + 0.5)).astype(F32)
    base, step = limits(low, high)
    scale = jnp.where(empty, 0.0, 1.0 / jnp.where(empty, 1.0, step))
    code = jnp.clip((x - base) * scale + 0.5, 0.0, LEVELS).astype(jnp.int32) - LEVELS // 2
    return code, low, high


def decode(code, low, high):
    base, step = limits(low, high)
    return base + (code.astype(jnp.int32) + LEVELS // 2).astype(F32) * step


def put_codes(ref, first, groups):
    table = []
    for x in groups:
        code, low, high = encode(x)
        ref[first : first + x.shape[0], :] = code.astype(jnp.int16)
        table += [low, high]
        first += x.shape[0]
    return table


def put_table(ref, at, table):
    row = lax.broadcasted_iota(jnp.int32, (TABLE, table[0].shape[1]), 0)
    out = jnp.zeros(row.shape, F32)
    for i, line in enumerate(table):
        out = jnp.where(row == i, line, out)
    ref[at : at + TABLE, :] = out.astype(jnp.int32).astype(jnp.int16)


def get_table(ref, at):
    return ref[at : at + TABLE, :].astype(jnp.int32).astype(F32)


def get_codes(ref, first, rows, group, table, entry):
    out = []
    for i in range(rows // group):
        low, high = table[entry : entry + 1, :], table[entry + 1 : entry + 2, :]
        out.append(decode(ref[first + i * group : first + (i + 1) * group, :], low, high))
        entry += 2
    return jnp.concatenate(out, axis=0)


def put_parts(ref, parts):
    groups = []
    for x in parts:
        group = min(BLOCK, x.shape[0])
        groups += [x[i : i + group] for i in range(0, x.shape[0], group)]
    table = put_codes(ref, 0, groups)
    put_table(ref, sum(x.shape[0] for x in parts), table)


def get_parts(ref, sizes):
    table = get_table(ref, sum(sizes))
    out, first, entry = [], 0, 0
    for rows in sizes:
        group = min(BLOCK, rows)
        out.append(get_codes(ref, first, rows, group, table, entry))
        first += rows
        entry += 2 * (rows // group)
    return out


def core_index():
    return lax.axis_index("term") & 1


def quad_index():
    return lax.axis_index("doc") & 3


def doc_bit(bit):
    return (lax.axis_index("doc") >> bit) & 1


def pack(gram, core):
    k = gram.shape[0]
    h, q = k // 2, k // 4
    e = q // 2
    if core == 0:
        diag, off = gram[:h, :h], gram[:q, h:]
    else:
        diag, off = gram[h:, h:], gram[q:h, h:]
    top = jnp.concatenate([diag[:q], diag[q:]], axis=1)
    low = jnp.concatenate([off[:e], off[e:]], axis=1)
    return jnp.concatenate([top, low], axis=0)


def unpack(one, two):
    k = one.shape[1]
    h, q = k // 2, k // 4
    e = q // 2

    def parts(p):
        diag = jnp.concatenate([p[:q, :h], p[:q, h:]], axis=0)
        off = jnp.concatenate([p[q : q + e, :h], p[q : q + e, h:]], axis=0)
        return diag, off

    diag_one, off_one = parts(one)
    diag_two, off_two = parts(two)
    off = jnp.concatenate([off_one, off_two], axis=0)
    upper = jnp.concatenate([diag_one, off], axis=1)
    lower = jnp.concatenate([off.T, diag_two], axis=1)
    return jnp.concatenate([upper, lower], axis=0)


def pick(core, one, two):
    return jnp.where(core == 0, one, two)


def mask_rows(pattern, half, cols):
    blocks = cols // BLOCK
    lane = lax.broadcasted_iota(jnp.int32, (pattern.shape[0], cols), 1) // BLOCK
    mask = jnp.zeros((pattern.shape[0], cols), F32)
    for c in range(blocks):
        column = pick(half, pattern[:, c : c + 1], pattern[:, blocks + c : blocks + c + 1])
        mask = jnp.where(lane == c, column.astype(F32), mask)
    return mask


def masked_piece(tile_ref, mask, piece, rows):
    out = []
    for r in range(rows // BLOCK):
        first = piece * rows + r * BLOCK
        line = mask[first // BLOCK : first // BLOCK + 1, :].astype(BF16)
        out.append(tile_ref[first : first + BLOCK, :] * line)
    return jnp.concatenate(out, axis=0)


def load_body(m, w, wt, send, keep, own, other, w_all, sems):
    core = core_index()
    terms, cols = own.shape
    k = w.shape[1]
    rows = terms // PIECES
    columns = lambda side: pl.ds(pl.multiple_of(side * cols, cols), cols)
    copies = []
    for i in range(PIECES):
        part = pl.ds(i * rows, rows)
        copies.append(pltpu.make_async_copy(w.at[part, :], w_all.at[part, :], sems.at[i]))
    copies.append(pltpu.make_async_copy(m.at[:, columns(1 - core)], other, sems.at[PIECES]))
    copies.append(pltpu.make_async_copy(m.at[:, columns(core)], own, sems.at[PIECES + 1]))
    for copy in copies:
        copy.start()
    gram = jnp.zeros((k, k), F32)
    for i in range(PIECES):
        part = slice(i * rows, (i + 1) * rows)
        copies[i].wait()
        piece = w_all[part, :]
        flipped = piece.T
        wt[:, part] = flipped
        gram += nn(flipped, piece)
    one, two = pack(gram, 0), pack(gram, 1)
    send[...] = pick(core, two, one)
    keep[...] = pick(core, one, two)
    for copy in copies[PIECES:]:
        copy.wait()


def half_h_body(h, out):
    cols = out.shape[1]
    out[...] = h[:, pl.ds(pl.multiple_of(core_index() * cols, cols), cols)]


def numer_body(half, pattern, wt, *refs, other):
    out, masked = refs[-2:]
    side = 1 - core_index() if other else core_index()
    terms, cols = half.shape
    rows = terms // PIECES
    mask = mask_rows(pattern[...], side, cols)
    for i in range(PIECES):
        part = slice(i * rows, (i + 1) * rows)
        tile = masked_piece(half, mask, i, rows)
        masked[part, :] = tile
        product = nn(wt[:, part], tile)
        if i == 0:
            out[...] = product
        else:
            out[...] += product


def add_body(a, b, out):
    out[...] = a[...] + b[...]


def round_add_body(a, b, out):
    out[...] = (a[...] + b[...]).astype(BF16)


def code_sum_body(a, b, out):
    rows = a.shape[0]
    table = put_codes(out, 0, [a[...] + b[...]])
    put_table(out, rows, table)


def new_h_body(mine, other, gram_mine, gram_other, h, out):
    core = core_index()
    a, b = gram_mine[...], gram_other[...]
    gram = unpack(pick(core, a, b), pick(core, b, a))
    old = h[...]
    rows = h.shape[0]
    total = None
    for ref in (mine, other):
        part = get_codes(ref, 0, rows, rows, get_table(ref, rows), 0)
        total = part if total is None else total + part
    out[...] = (old.astype(F32) * total / nn(gram, old)).astype(BF16)


def first_w_body(masked, h, out):
    step = masked.shape[0] // 2
    for r in range(2):
        part = slice(r * step, (r + 1) * step)
        out[part, :] = nt(masked[part, :], h[...])


def piece_of(masked, part, h, index, size):
    start = pl.multiple_of(index * size, size)
    return part[pl.ds(start, size), :] + nt(masked[pl.ds(start, size), :], h[...])


def first_send_body(masked, part, h, h_own, out, gram_out, *, away):
    size = masked.shape[0] // 4
    gram = nt(h[...], h[...]) + nt(h_own[...], h_own[...])
    gram = pick(core_index(), pack(gram, 0), pack(gram, 1))
    gram_out[...] = gram
    put_parts(out, [piece_of(masked, part, h, quad_index() ^ away, size), gram])


def send_body(masked, part, h, gram, out, *, away):
    size = masked.shape[0] // 4
    put_parts(out, [piece_of(masked, part, h, quad_index() ^ away, size), gram[...]])


def keep_rows_body(masked, part, h, out):
    out[...] = piece_of(masked, part, h, quad_index(), out.shape[0])


def new_h_out_body(h, h_own, out):
    core, cols = core_index(), h.shape[1]
    out[:, pl.ds(pl.multiple_of((1 - core) * cols, cols), cols)] = h[...]
    out[:, pl.ds(pl.multiple_of(core * cols, cols), cols)] = h_own[...]


def quad_sum_body(keep, own, one, two, three, *outs, pk, bit, last):
    size = keep.shape[0]
    rows, gram = zip(*[get_parts(ref, (size, pk)) for ref in (one, two, three)])
    gram_own = get_parts(own, (size, pk))[1]
    total = (keep[...] + rows[0]) + (rows[1] + rows[2])
    store_step(total, (gram_own + gram[0]) + (gram[1] + gram[2]), outs, bit, last)


def step_sum_body(keep, sent, got, *outs, pk, bit, last):
    size = keep.shape[0]
    rows, gram = get_parts(got, (size, pk))
    store_step(keep[...] + rows, get_parts(sent, (size, pk))[1] + gram, outs, bit, last)


def store_step(rows, gram, outs, bit, last):
    if last:
        put_parts(outs[0], [rows, gram])
        return
    half = rows.shape[0] // 2
    low, high = rows[:half], rows[half:]
    side = doc_bit(bit)
    put_parts(outs[0], [pick(side, high, low), gram])
    outs[1][...] = pick(side, low, high)


def gram_h_body(sent, got, out, *, size):
    pk = out.shape[0]
    out[...] = (get_parts(sent, (size, pk))[1] + get_parts(got, (size, pk))[1]).astype(BF16)


def new_w_body(gram_mine, gram_other, w, sent, got, out):
    core = core_index()
    one, two = gram_mine[...], gram_other[...]
    gram = unpack(pick(core, one, two), pick(core, two, one))
    size, pk = w.shape[0], one.shape[0]
    total = get_parts(sent, (size, pk))[0] + get_parts(got, (size, pk))[0]
    old = w[...]
    out[...] = (old.astype(F32) * total / nn(old, gram)).astype(BF16)


def new_w_out_body(own, one, two, three, out):
    size = own.shape[0]
    for away, ref in enumerate((own, one, two, three)):
        out[pl.ds(pl.multiple_of((quad_index() ^ away) * size, size), size), :] = ref[...]


def swap(x, axis, size, away):
    return lax.ppermute(x, axis, [(i, i ^ away) for i in range(size)])


def join(bit, mine, other):
    return jnp.concatenate([jnp.where(bit == 0, mine, other), jnp.where(bit == 0, other, mine)], axis=0)


def on_device(m, pattern, w, h, *, n_doc, n_term):
    return update(m, pattern, w, h, n_doc, n_term)


def update(m, pattern, w, h, n_doc, n_term):
    terms, docs = m.shape
    k = w.shape[1]
    half = docs // 2
    pk = 3 * k // 8
    bits = n_doc.bit_length() - 1
    term_bits = n_term.bit_length() - 1

    def over_term(x, bit):
        return swap(x, "term", n_term, 1 << bit)

    def over_doc(x, away):
        return swap(x, "doc", n_doc, away)

    flops = terms * docs * k
    moved = 2 * terms * docs

    side = like(terms, half, dtype=BF16)
    wt, g_send, g_keep, own, other = call(
        load_body,
        (like(k, terms, dtype=BF16), like(pk, k), like(pk, k), side, side),
        (m, w),
        hbm=(0, 1),
        scratch=(pltpu.VMEM((terms, k), BF16), pltpu.SemaphoreType.DMA((PIECES + 2,))),
        limit=LIMIT,
    )
    g_got = over_term(g_send, 0)

    def numer(half_m, is_other, *after):
        body = functools.partial(numer_body, other=is_other)
        return call(body, (like(k, half), side), (half_m, pattern, wt, *after), flops=flops, moved=moved)

    n_send, masked_other = numer(other, True)
    n_got = over_term(n_send, 0)
    g_sum = call(add_body, like(pk, k), (g_keep, g_got))
    for bit in range(1, term_bits - 1):
        g_sum = g_sum + over_term(g_sum, bit)
    g_far = over_term(g_sum, term_bits - 1)
    n_keep, masked_own = numer(own, False, g_sum)
    h_old = call(half_h_body, like(k, half, dtype=BF16), (h,))
    for bit in range(1, term_bits - 1):
        n_keep = call(add_body, like(k, half), (n_keep, n_got))
        n_got = over_term(n_keep, bit)
    n_sum = call(code_sum_body, like(k + TABLE, half, dtype=jnp.int16), (n_keep, n_got))
    n_far = over_term(n_sum, term_bits - 1)
    g_mine = call(round_add_body, like(pk, k, dtype=BF16), (g_sum, g_far))
    g_other = over_term(g_mine, 0)
    h_own = call(new_h_body, like(k, half, dtype=BF16), (n_sum, n_far, g_mine, g_other, h_old))
    h_other = over_term(h_own, 0)

    part = call(first_w_body, like(terms, k), (masked_own, h_own), flops=flops, moved=moved)
    size = terms // 4
    payload = lambda rows: like(rows + pk + TABLE, k, dtype=jnp.int16)
    costs = dict(flops=flops // 4, moved=moved // 4)
    sent, got = {}, {}
    body = functools.partial(first_send_body, away=3)
    sent[3], gram = call(body, (payload(size), like(pk, k)), (masked_other, part, h_other, h_own), **costs)
    for away in (1, 2):
        body = functools.partial(send_body, away=away)
        sent[away] = call(body, payload(size), (masked_other, part, h_other, gram), **costs)
    for away in (3, 1, 2):
        got[away] = over_doc(sent[away], away)
    keep = call(keep_rows_body, like(size, k), (masked_other, part, h_other), **costs)
    new_h = call(new_h_out_body, like(k, docs, dtype=BF16), (h_other, h_own))
    ends = (sent[1], got[1], got[2], got[3])
    for bit in range(2, bits):
        last = bit == bits - 1
        body = quad_sum_body if bit == 2 else step_sum_body
        rows = size if last else size // 2
        outs = (payload(rows),) if last else (payload(rows), like(rows, k))
        moving, *kept = call(functools.partial(body, pk=pk, bit=bit, last=last), outs, (keep, *ends))
        keep, size = (kept[0] if kept else None), rows
        ends = (moving, over_doc(moving, 1 << bit))
    g_mine = call(functools.partial(gram_h_body, size=size), like(pk, k, dtype=BF16), ends)
    g_other = over_term(g_mine, 0)
    start = quad_index() * (terms // 4)
    for bit in range(2, bits - 1):
        start += doc_bit(bit) * (terms // 4 >> (bit - 1))
    old = lax.dynamic_slice_in_dim(w, start, size, 0)
    share = call(new_w_body, like(size, k, dtype=BF16), (g_mine, g_other, old, *ends))
    for bit in reversed(range(2, bits - 1)):
        share = join(doc_bit(bit), share, over_doc(share, 1 << bit))
    shares = {away: over_doc(share, away) for away in (3, 1, 2)}
    new_w = call(new_w_out_body, like(terms, k, dtype=BF16), (share, shares[1], shares[2], shares[3]))
    return new_w, new_h


def solution(mesh):
    sizes = dict(mesh.shape)
    return jax.shard_map(
        functools.partial(on_device, n_doc=sizes["doc"], n_term=sizes["term"]),
        mesh=mesh,
        in_specs=(P("term", "doc"), P("term", "doc"), P("term", None), P(None, "doc")),
        out_specs=(P("term", None), P(None, "doc")),
        check_vma=False,
    )
```

```python
import functools

import jax
import jax.numpy as jnp
from jax import lax
from jax.experimental import pallas as pl
from jax.experimental.pallas import tpu as pltpu
from jax.sharding import PartitionSpec as P


BLOCK = 128
F32 = jnp.float32
BF16 = jnp.bfloat16
VMEM = pl.BlockSpec(memory_space=pltpu.VMEM)
HBM = pl.BlockSpec(memory_space=pltpu.HBM)
PIECES = 4
TABLE = 16


def nt(a, b):
    return lax.dot_general(a, b, (((1,), (1,)), ((), ())), preferred_element_type=F32)


def nn(a, b):
    return lax.dot_general(a, b, (((1,), (0,)), ((), ())), preferred_element_type=F32)


def call(body, out, args, hbm=(), scratch=(), flops=1 << 20, moved=1 << 20, limit=24 << 20):
    return pl.pallas_call(
        body,
        out_shape=out,
        in_specs=[HBM if i in hbm else VMEM for i in range(len(args))],
        out_specs=jax.tree.map(lambda _: VMEM, out),
        scratch_shapes=list(scratch),
        compiler_params=pltpu.CompilerParams(vmem_limit_bytes=limit),
        cost_estimate=pl.CostEstimate(flops=flops, bytes_accessed=moved, transcendentals=0),
    )(*args)


def like(*shape, dtype=F32):
    return jax.ShapeDtypeStruct(shape, dtype)


LEVELS = 65534
PER_OCTAVE = 512
EMPTY = -32768


def limits(low, high):
    empty = high == EMPTY
    least = jnp.where(empty, 0.0, jnp.exp2(low * (1.0 / PER_OCTAVE)))
    step = jnp.where(empty, 0.0, (jnp.exp2(high * (1.0 / PER_OCTAVE)) - least) * (1.0 / LEVELS))
    return least, step


def encode(x):
    least = jnp.min(x, axis=0, keepdims=True)
    most = jnp.max(x, axis=0, keepdims=True)
    octave = lambda v: jnp.log2(jnp.maximum(v, 1e-18)) * PER_OCTAVE
    empty = most <= 0.0
    low = jnp.where(empty, EMPTY, jnp.floor(octave(least) - 0.5)).astype(F32)
    high = jnp.where(empty, EMPTY, jnp.ceil(octave(most) + 0.5)).astype(F32)
    base, step = limits(low, high)
    scale = jnp.where(empty, 0.0, 1.0 / jnp.where(empty, 1.0, step))
    code = jnp.clip((x - base) * scale + 0.5, 0.0, LEVELS).astype(jnp.int32) - LEVELS // 2
    return code, low, high


def decode(code, low, high):
    base, step = limits(low, high)
    return base + (code.astype(jnp.int32) + LEVELS // 2).astype(F32) * step


def put_codes(ref, first, groups):
    table = []
    for x in groups:
        code, low, high = encode(x)
        ref[first : first + x.shape[0], :] = code.astype(jnp.int16)
        table += [low, high]
        first += x.shape[0]
    return table


def put_table(ref, at, table):
    row = lax.broadcasted_iota(jnp.int32, (TABLE, table[0].shape[1]), 0)
    out = jnp.zeros(row.shape, F32)
    for i, line in enumerate(table):
        out = jnp.where(row == i, line, out)
    ref[at : at + TABLE, :] = out.astype(jnp.int32).astype(jnp.int16)


def get_table(ref, at):
    return ref[at : at + TABLE, :].astype(jnp.int32).astype(F32)


def get_codes(ref, first, rows, group, table, entry):
    out = []
    for i in range(rows // group):
        low, high = table[entry : entry + 1, :], table[entry + 1 : entry + 2, :]
        out.append(decode(ref[first + i * group : first + (i + 1) * group, :], low, high))
        entry += 2
    return jnp.concatenate(out, axis=0)


def put_parts(ref, parts):
    groups = []
    for x in parts:
        group = min(BLOCK, x.shape[0])
        groups += [x[i : i + group] for i in range(0, x.shape[0], group)]
    table = put_codes(ref, 0, groups)
    put_table(ref, sum(x.shape[0] for x in parts), table)


def get_parts(ref, sizes):
    table = get_table(ref, sum(sizes))
    out, first, entry = [], 0, 0
    for rows in sizes:
        group = min(BLOCK, rows)
        out.append(get_codes(ref, first, rows, group, table, entry))
        first += rows
        entry += 2 * (rows // group)
    return out


def core_index():
    return lax.axis_index("term") & 1


def quad_index():
    return lax.axis_index("doc") & 3


def doc_bit(bit):
    return (lax.axis_index("doc") >> bit) & 1


def pack(gram, core):
    k = gram.shape[0]
    h, q = k // 2, k // 4
    e = q // 2
    if core == 0:
        diag, off = gram[:h, :h], gram[:q, h:]
    else:
        diag, off = gram[h:, h:], gram[q:h, h:]
    top = jnp.concatenate([diag[:q], diag[q:]], axis=1)
    low = jnp.concatenate([off[:e], off[e:]], axis=1)
    return jnp.concatenate([top, low], axis=0)


def unpack(one, two):
    k = one.shape[1]
    h, q = k // 2, k // 4
    e = q // 2

    def parts(p):
        diag = jnp.concatenate([p[:q, :h], p[:q, h:]], axis=0)
        off = jnp.concatenate([p[q : q + e, :h], p[q : q + e, h:]], axis=0)
        return diag, off

    diag_one, off_one = parts(one)
    diag_two, off_two = parts(two)
    off = jnp.concatenate([off_one, off_two], axis=0)
    upper = jnp.concatenate([diag_one, off], axis=1)
    lower = jnp.concatenate([off.T, diag_two], axis=1)
    return jnp.concatenate([upper, lower], axis=0)


def pick(core, one, two):
    return jnp.where(core == 0, one, two)


def mask_rows(pattern, half, cols):
    blocks = cols // BLOCK
    lane = lax.broadcasted_iota(jnp.int32, (pattern.shape[0], cols), 1) // BLOCK
    mask = jnp.zeros((pattern.shape[0], cols), F32)
    for c in range(blocks):
        column = pick(half, pattern[:, c : c + 1], pattern[:, blocks + c : blocks + c + 1])
        mask = jnp.where(lane == c, column.astype(F32), mask)
    return mask


def masked_piece(tile_ref, mask, piece, rows):
    out = []
    for r in range(rows // BLOCK):
        first = piece * rows + r * BLOCK
        line = mask[first // BLOCK : first // BLOCK + 1, :].astype(BF16)
        out.append(tile_ref[first : first + BLOCK, :] * line)
    return jnp.concatenate(out, axis=0)


def gram_w_body(w, wt, send, keep):
    core = core_index()
    flipped = w[...].T
    wt[...] = flipped
    gram = nn(flipped, w[...])
    one, two = pack(gram, 0), pack(gram, 1)
    send[...] = pick(core, two, one)
    keep[...] = pick(core, one, two)


def half_h_body(h, out):
    cols = out.shape[1]
    out[...] = h[:, pl.ds(pl.multiple_of(core_index() * cols, cols), cols)]


def numer_body(m, pattern, wt, *refs, other):
    out, masked = refs[-2:]
    side = 1 - core_index() if other else core_index()
    terms, cols = masked.shape
    rows = terms // PIECES
    half = m.at[:, pl.ds(pl.multiple_of(side * cols, cols), cols)]
    mask = mask_rows(pattern[...], side, cols)
    for i in range(PIECES):
        part = slice(i * rows, (i + 1) * rows)
        tile = masked_piece(half, mask, i, rows)
        masked[part, :] = tile
        product = nn(wt[:, part], tile)
        if i == 0:
            out[...] = product
        else:
            out[...] += product


def add_body(a, b, out):
    out[...] = a[...] + b[...]


def round_sum_body(a, b, out):
    rows = out.shape[0]
    out[...] = (get_parts(a, (rows,))[0] + get_parts(b, (rows,))[0]).astype(BF16)


def code_sum_body(a, b, out):
    total = a[...] + b[...]
    put_table(out, total.shape[0], put_codes(out, 0, [total]))


def new_h_body(mine, other, gram_mine, gram_other, h, out):
    core = core_index()
    a, b = gram_mine[...], gram_other[...]
    gram = unpack(pick(core, a, b), pick(core, b, a))
    old = h[...]
    rows = h.shape[0]
    total = None
    for ref in (mine, other):
        part = get_codes(ref, 0, rows, rows, get_table(ref, rows), 0)
        total = part if total is None else total + part
    out[...] = (old.astype(F32) * total / nn(gram, old)).astype(BF16)


def first_w_body(masked, h, out):
    step = masked.shape[0] // 2
    for r in range(2):
        part = slice(r * step, (r + 1) * step)
        out[part, :] = nt(masked[part, :], h[...])


def piece_of(masked, part, h, index, size):
    start = pl.multiple_of(index * size, size)
    return part[pl.ds(start, size), :] + nt(masked[pl.ds(start, size), :], h[...])


def first_send_body(masked, part, h, h_own, out, gram_out, *, away):
    size = masked.shape[0] // 4
    gram = nt(h[...], h[...]) + nt(h_own[...], h_own[...])
    gram = pick(core_index(), pack(gram, 0), pack(gram, 1))
    gram_out[...] = gram
    put_parts(out, [piece_of(masked, part, h, quad_index() ^ away, size), gram])


def send_body(masked, part, h, gram, out, *, away):
    size = masked.shape[0] // 4
    put_parts(out, [piece_of(masked, part, h, quad_index() ^ away, size), gram[...]])


def keep_rows_body(masked, part, h, out):
    out[...] = piece_of(masked, part, h, quad_index(), out.shape[0])


def new_h_out_body(h, h_own, out):
    core, cols = core_index(), h.shape[1]
    out[:, pl.ds(pl.multiple_of((1 - core) * cols, cols), cols)] = h[...]
    out[:, pl.ds(pl.multiple_of(core * cols, cols), cols)] = h_own[...]


def quad_sum_body(keep, own, one, two, three, *outs, pk, bit, last):
    size = keep.shape[0]
    rows, gram = zip(*[get_parts(ref, (size, pk)) for ref in (one, two, three)])
    gram_own = get_parts(own, (size, pk))[1]
    total = (keep[...] + rows[0]) + (rows[1] + rows[2])
    store_step(total, (gram_own + gram[0]) + (gram[1] + gram[2]), outs, bit, last)


def step_sum_body(keep, sent, got, *outs, pk, bit, last):
    size = keep.shape[0]
    rows, gram = get_parts(got, (size, pk))
    store_step(keep[...] + rows, get_parts(sent, (size, pk))[1] + gram, outs, bit, last)


def store_step(rows, gram, outs, bit, last):
    if last:
        put_parts(outs[0], [rows, gram])
        return
    half = rows.shape[0] // 2
    low, high = rows[:half], rows[half:]
    side = doc_bit(bit)
    put_parts(outs[0], [pick(side, high, low), gram])
    outs[1][...] = pick(side, low, high)


def gram_h_body(sent, got, out, *, size):
    pk = out.shape[0]
    out[...] = (get_parts(sent, (size, pk))[1] + get_parts(got, (size, pk))[1]).astype(BF16)


def new_w_body(gram_mine, gram_other, w, sent, got, out):
    core = core_index()
    one, two = gram_mine[...], gram_other[...]
    gram = unpack(pick(core, one, two), pick(core, two, one))
    size, pk = w.shape[0], one.shape[0]
    total = get_parts(sent, (size, pk))[0] + get_parts(got, (size, pk))[0]
    old = w[...]
    out[...] = (old.astype(F32) * total / nn(old, gram)).astype(BF16)


def new_w_out_body(own, one, two, three, out):
    size = own.shape[0]
    for away, ref in enumerate((own, one, two, three)):
        out[pl.ds(pl.multiple_of((quad_index() ^ away) * size, size), size), :] = ref[...]


def swap(x, axis, size, away):
    return lax.ppermute(x, axis, [(i, i ^ away) for i in range(size)])


def join(bit, mine, other):
    return jnp.concatenate([jnp.where(bit == 0, mine, other), jnp.where(bit == 0, other, mine)], axis=0)


def on_device(m, pattern, w, h, *, n_doc, n_term):
    return update(m, pattern, w, h, n_doc, n_term)


def update(m, pattern, w, h, n_doc, n_term):
    terms, docs = m.shape
    k = w.shape[1]
    half = docs // 2
    pk = 3 * k // 8
    bits = n_doc.bit_length() - 1
    term_bits = n_term.bit_length() - 1

    def over_term(x, bit):
        return swap(x, "term", n_term, 1 << bit)

    def over_doc(x, away):
        return swap(x, "doc", n_doc, away)

    flops = terms * docs * k
    moved = 2 * terms * docs

    side = like(terms, half, dtype=BF16)
    wt, g_send, g_keep = call(
        gram_w_body, (like(k, terms, dtype=BF16), like(pk, k), like(pk, k)), (w,), flops=32 * flops, moved=moved
    )
    g_got = over_term(g_send, 0)

    def numer(is_other, *after):
        body = functools.partial(numer_body, other=is_other)
        return call(body, (like(k, half), side), (m, pattern, wt, *after), flops=flops, moved=moved)

    n_send, masked_other = numer(True)
    n_got = over_term(n_send, 0)
    for bit in range(1, term_bits - 1):
        g_keep = call(add_body, like(pk, k), (g_keep, g_got))
        g_got = over_term(g_keep, bit)
    g_sum = call(code_sum_body, like(pk + TABLE, k, dtype=jnp.int16), (g_keep, g_got))
    g_far = over_term(g_sum, term_bits - 1)
    n_keep, masked_own = numer(False, g_sum)
    h_old = call(half_h_body, like(k, half, dtype=BF16), (h,))
    for bit in range(1, term_bits - 1):
        n_keep = call(add_body, like(k, half), (n_keep, n_got))
        n_got = over_term(n_keep, bit)
    n_sum = call(code_sum_body, like(k + TABLE, half, dtype=jnp.int16), (n_keep, n_got))
    n_far = over_term(n_sum, term_bits - 1)
    g_mine = call(round_sum_body, like(pk, k, dtype=BF16), (g_sum, g_far))
    g_other = over_term(g_mine, 0)
    h_own = call(new_h_body, like(k, half, dtype=BF16), (n_sum, n_far, g_mine, g_other, h_old))
    h_other = over_term(h_own, 0)

    part = call(first_w_body, like(terms, k), (masked_own, h_own), flops=flops, moved=moved)
    size = terms // 4
    payload = lambda rows: like(rows + pk + TABLE, k, dtype=jnp.int16)
    costs = dict(flops=flops // 4, moved=moved // 4)
    sent, got = {}, {}
    body = functools.partial(first_send_body, away=3)
    sent[3], gram = call(body, (payload(size), like(pk, k)), (masked_other, part, h_other, h_own), **costs)
    for away in (1, 2):
        body = functools.partial(send_body, away=away)
        sent[away] = call(body, payload(size), (masked_other, part, h_other, gram), **costs)
    for away in (3, 1, 2):
        got[away] = over_doc(sent[away], away)
    keep = call(keep_rows_body, like(size, k), (masked_other, part, h_other), **costs)
    new_h = call(new_h_out_body, like(k, docs, dtype=BF16), (h_other, h_own))
    ends = (sent[1], got[1], got[2], got[3])
    for bit in range(2, bits):
        last = bit == bits - 1
        body = quad_sum_body if bit == 2 else step_sum_body
        rows = size if last else size // 2
        outs = (payload(rows),) if last else (payload(rows), like(rows, k))
        moving, *kept = call(functools.partial(body, pk=pk, bit=bit, last=last), outs, (keep, *ends))
        keep, size = (kept[0] if kept else None), rows
        ends = (moving, over_doc(moving, 1 << bit))
    g_mine = call(functools.partial(gram_h_body, size=size), like(pk, k, dtype=BF16), ends)
    g_other = over_term(g_mine, 0)
    start = quad_index() * (terms // 4)
    for bit in range(2, bits - 1):
        start += doc_bit(bit) * (terms // 4 >> (bit - 1))
    old = lax.dynamic_slice_in_dim(w, start, size, 0)
    share = call(new_w_body, like(size, k, dtype=BF16), (g_mine, g_other, old, *ends))
    for bit in reversed(range(2, bits - 1)):
        share = join(doc_bit(bit), share, over_doc(share, 1 << bit))
    shares = {away: over_doc(share, away) for away in (3, 1, 2)}
    new_w = call(new_w_out_body, like(terms, k, dtype=BF16), (share, shares[1], shares[2], shares[3]))
    return new_w, new_h


def solution(mesh):
    sizes = dict(mesh.shape)
    return jax.shard_map(
        functools.partial(on_device, n_doc=sizes["doc"], n_term=sizes["term"]),
        mesh=mesh,
        in_specs=(P("term", "doc"), P("term", "doc"), P("term", None), P(None, "doc")),
        out_specs=(P("term", None), P(None, "doc")),
        check_vma=False,
    )
```

```python
import functools

import jax
import jax.numpy as jnp
from jax import lax
from jax.experimental import pallas as pl
from jax.experimental.pallas import tpu as pltpu
from jax.sharding import PartitionSpec as P


BLOCK = 128
F32 = jnp.float32
BF16 = jnp.bfloat16
VMEM = pl.BlockSpec(memory_space=pltpu.VMEM)
HBM = pl.BlockSpec(memory_space=pltpu.HBM)
PIECES = 4
TABLE = 16


def nt(a, b):
    return lax.dot_general(a, b, (((1,), (1,)), ((), ())), preferred_element_type=F32)


def nn(a, b):
    return lax.dot_general(a, b, (((1,), (0,)), ((), ())), preferred_element_type=F32)


def call(body, out, args, hbm=(), scratch=(), flops=1 << 20, moved=1 << 20, limit=24 << 20):
    return pl.pallas_call(
        body,
        out_shape=out,
        in_specs=[HBM if i in hbm else VMEM for i in range(len(args))],
        out_specs=jax.tree.map(lambda _: VMEM, out),
        scratch_shapes=list(scratch),
        compiler_params=pltpu.CompilerParams(vmem_limit_bytes=limit),
        cost_estimate=pl.CostEstimate(flops=flops, bytes_accessed=moved, transcendentals=0),
    )(*args)


def like(*shape, dtype=F32):
    return jax.ShapeDtypeStruct(shape, dtype)


LEVELS = 65534
PER_OCTAVE = 512
EMPTY = -32768


def limits(low, high):
    empty = high == EMPTY
    least = jnp.where(empty, 0.0, jnp.exp2(low * (1.0 / PER_OCTAVE)))
    step = jnp.where(empty, 0.0, (jnp.exp2(high * (1.0 / PER_OCTAVE)) - least) * (1.0 / LEVELS))
    return least, step


def encode(x):
    least = jnp.min(x, axis=0, keepdims=True)
    most = jnp.max(x, axis=0, keepdims=True)
    octave = lambda v: jnp.log2(jnp.maximum(v, 1e-18)) * PER_OCTAVE
    empty = most <= 0.0
    low = jnp.where(empty, EMPTY, jnp.floor(octave(least) - 0.5)).astype(F32)
    high = jnp.where(empty, EMPTY, jnp.ceil(octave(most) + 0.5)).astype(F32)
    base, step = limits(low, high)
    scale = jnp.where(empty, 0.0, 1.0 / jnp.where(empty, 1.0, step))
    code = jnp.clip((x - base) * scale + 0.5, 0.0, LEVELS).astype(jnp.int32) - LEVELS // 2
    return code, low, high


def decode(code, low, high):
    base, step = limits(low, high)
    return base + (code.astype(jnp.int32) + LEVELS // 2).astype(F32) * step


def put_codes(ref, first, groups):
    table = []
    for x in groups:
        code, low, high = encode(x)
        ref[first : first + x.shape[0], :] = code.astype(jnp.int16)
        table += [low, high]
        first += x.shape[0]
    return table


def put_table(ref, at, table):
    row = lax.broadcasted_iota(jnp.int32, (TABLE, table[0].shape[1]), 0)
    out = jnp.zeros(row.shape, F32)
    for i, line in enumerate(table):
        out = jnp.where(row == i, line, out)
    ref[at : at + TABLE, :] = out.astype(jnp.int32).astype(jnp.int16)


def get_table(ref, at):
    return ref[at : at + TABLE, :].astype(jnp.int32).astype(F32)


def get_codes(ref, first, rows, group, table, entry):
    out = []
    for i in range(rows // group):
        low, high = table[entry : entry + 1, :], table[entry + 1 : entry + 2, :]
        out.append(decode(ref[first + i * group : first + (i + 1) * group, :], low, high))
        entry += 2
    return jnp.concatenate(out, axis=0)


def put_parts(ref, parts):
    groups = []
    for x in parts:
        group = min(BLOCK, x.shape[0])
        groups += [x[i : i + group] for i in range(0, x.shape[0], group)]
    table = put_codes(ref, 0, groups)
    put_table(ref, sum(x.shape[0] for x in parts), table)


def get_parts(ref, sizes):
    table = get_table(ref, sum(sizes))
    out, first, entry = [], 0, 0
    for rows in sizes:
        group = min(BLOCK, rows)
        out.append(get_codes(ref, first, rows, group, table, entry))
        first += rows
        entry += 2 * (rows // group)
    return out


def core_index():
    return lax.axis_index("term") & 1


def quad_index():
    return lax.axis_index("doc") & 3


def doc_bit(bit):
    return (lax.axis_index("doc") >> bit) & 1


def pack(gram, core):
    k = gram.shape[0]
    h, q = k // 2, k // 4
    e = q // 2
    if core == 0:
        diag, off = gram[:h, :h], gram[:q, h:]
    else:
        diag, off = gram[h:, h:], gram[q:h, h:]
    top = jnp.concatenate([diag[:q], diag[q:]], axis=1)
    low = jnp.concatenate([off[:e], off[e:]], axis=1)
    return jnp.concatenate([top, low], axis=0)


def unpack(one, two):
    k = one.shape[1]
    h, q = k // 2, k // 4
    e = q // 2

    def parts(p):
        diag = jnp.concatenate([p[:q, :h], p[:q, h:]], axis=0)
        off = jnp.concatenate([p[q : q + e, :h], p[q : q + e, h:]], axis=0)
        return diag, off

    diag_one, off_one = parts(one)
    diag_two, off_two = parts(two)
    off = jnp.concatenate([off_one, off_two], axis=0)
    upper = jnp.concatenate([diag_one, off], axis=1)
    lower = jnp.concatenate([off.T, diag_two], axis=1)
    return jnp.concatenate([upper, lower], axis=0)


def pick(core, one, two):
    return jnp.where(core == 0, one, two)


def mask_rows(pattern, half, cols):
    blocks = cols // BLOCK
    lane = lax.broadcasted_iota(jnp.int32, (pattern.shape[0], cols), 1) // BLOCK
    mask = jnp.zeros((pattern.shape[0], cols), F32)
    for c in range(blocks):
        column = pick(half, pattern[:, c : c + 1], pattern[:, blocks + c : blocks + c + 1])
        mask = jnp.where(lane == c, column.astype(F32), mask)
    return mask


def masked_piece(tile_ref, mask, piece, rows):
    out = []
    for r in range(rows // BLOCK):
        first = piece * rows + r * BLOCK
        line = mask[first // BLOCK : first // BLOCK + 1, :].astype(BF16)
        out.append(tile_ref[first : first + BLOCK, :] * line)
    return jnp.concatenate(out, axis=0)


def gram_w_body(w, wt, send, keep):
    core = core_index()
    flipped = w[...].T
    wt[...] = flipped
    gram = nn(flipped, w[...])
    one, two = pack(gram, 0), pack(gram, 1)
    send[...] = pick(core, two, one)
    keep[...] = pick(core, one, two)


def half_h_body(h, out):
    cols = out.shape[1]
    out[...] = h[:, pl.ds(pl.multiple_of(core_index() * cols, cols), cols)]


def numer_body(m, pattern, wt, *refs, other):
    out, masked = refs[-2:]
    side = 1 - core_index() if other else core_index()
    terms, cols = masked.shape
    rows = terms // PIECES
    half = m.at[:, pl.ds(pl.multiple_of(side * cols, cols), cols)]
    mask = mask_rows(pattern[...], side, cols)
    for i in range(PIECES):
        part = slice(i * rows, (i + 1) * rows)
        tile = masked_piece(half, mask, i, rows)
        masked[part, :] = tile
        product = nn(wt[:, part], tile)
        if i == 0:
            out[...] = product
        else:
            out[...] += product


def add_body(a, b, out):
    out[...] = a[...] + b[...]


def round_add_body(a, b, out):
    out[...] = (a[...] + b[...]).astype(BF16)


def code_sum_body(a, b, out):
    total = a[...] + b[...]
    put_table(out, total.shape[0], put_codes(out, 0, [total]))


def new_h_body(mine, other, gram_mine, gram_other, h, out):
    core = core_index()
    a, b = gram_mine[...], gram_other[...]
    gram = unpack(pick(core, a, b), pick(core, b, a))
    old = h[...]
    rows = h.shape[0]
    total = None
    for ref in (mine, other):
        part = get_codes(ref, 0, rows, rows, get_table(ref, rows), 0)
        total = part if total is None else total + part
    out[...] = (old.astype(F32) * total / nn(gram, old)).astype(BF16)


def first_w_body(masked, h, out):
    step = masked.shape[0] // 2
    for r in range(2):
        part = slice(r * step, (r + 1) * step)
        out[part, :] = nt(masked[part, :], h[...])


def piece_of(masked, part, h, index, size):
    start = pl.multiple_of(index * size, size)
    return part[pl.ds(start, size), :] + nt(masked[pl.ds(start, size), :], h[...])


def send_body(masked, part, h, out, *, away):
    put_parts(out, [piece_of(masked, part, h, quad_index() ^ away, masked.shape[0] // 4)])


def keep_rows_body(masked, part, h, out):
    out[...] = piece_of(masked, part, h, quad_index(), out.shape[0])


def gram_h_body(h, h_own, out):
    gram = nt(h[...], h[...]) + nt(h_own[...], h_own[...])
    out[...] = pick(core_index(), pack(gram, 0), pack(gram, 1))


def gram_quad_body(own, one, two, three, out):
    out[...] = ((own[...] + one[...]) + (two[...] + three[...])).astype(BF16)


def new_h_out_body(h, h_own, out):
    core, cols = core_index(), h.shape[1]
    out[:, pl.ds(pl.multiple_of((1 - core) * cols, cols), cols)] = h[...]
    out[:, pl.ds(pl.multiple_of(core * cols, cols), cols)] = h_own[...]


def next_step_body(keep, *refs, bit, last):
    size = keep.shape[0]
    outs = refs[-1:] if last else refs[-2:]
    got = [get_parts(ref, (size,))[0] for ref in refs[: len(refs) - len(outs)]]
    rows = keep[...] + got[0]
    if len(got) > 1:
        rows += got[1] + got[2]
    if last:
        put_parts(outs[0], [rows])
        return
    half = size // 2
    low, high = rows[:half], rows[half:]
    side = doc_bit(bit)
    put_parts(outs[0], [pick(side, high, low)])
    outs[1][...] = pick(side, low, high)


def new_w_body(gram_mine, gram_other, w, sent, got, out):
    core = core_index()
    one, two = gram_mine[...], gram_other[...]
    gram = unpack(pick(core, one, two), pick(core, two, one))
    size = w.shape[0]
    total = get_parts(sent, (size,))[0] + get_parts(got, (size,))[0]
    old = w[...]
    out[...] = (old.astype(F32) * total / nn(old, gram)).astype(BF16)


def new_w_out_body(own, one, two, three, out):
    size = own.shape[0]
    for away, ref in enumerate((own, one, two, three)):
        out[pl.ds(pl.multiple_of((quad_index() ^ away) * size, size), size), :] = ref[...]


def swap(x, axis, size, away):
    return lax.ppermute(x, axis, [(i, i ^ away) for i in range(size)])


def join(bit, mine, other):
    return jnp.concatenate([jnp.where(bit == 0, mine, other), jnp.where(bit == 0, other, mine)], axis=0)


def on_device(m, pattern, w, h, *, n_doc, n_term):
    return update(m, pattern, w, h, n_doc, n_term)


def update(m, pattern, w, h, n_doc, n_term):
    terms, docs = m.shape
    k = w.shape[1]
    half = docs // 2
    pk = 3 * k // 8
    bits = n_doc.bit_length() - 1
    term_bits = n_term.bit_length() - 1

    def over_term(x, bit):
        return swap(x, "term", n_term, 1 << bit)

    def over_doc(x, away):
        return swap(x, "doc", n_doc, away)

    flops = terms * docs * k
    moved = 2 * terms * docs

    side = like(terms, half, dtype=BF16)
    wt, g_send, g_keep = call(
        gram_w_body, (like(k, terms, dtype=BF16), like(pk, k), like(pk, k)), (w,), flops=32 * flops, moved=moved
    )
    g_got = over_term(g_send, 0)

    def numer(is_other, *after):
        body = functools.partial(numer_body, other=is_other)
        return call(body, (like(k, half), side), (m, pattern, wt, *after), flops=flops, moved=moved)

    n_send, masked_other = numer(True)
    n_got = over_term(n_send, 0)
    for bit in range(1, term_bits - 1):
        g_keep = call(add_body, like(pk, k), (g_keep, g_got))
        g_got = over_term(g_keep, bit)
    g_sum = call(add_body, like(pk, k), (g_keep, g_got))
    g_far = over_term(g_sum, term_bits - 1)
    n_keep, masked_own = numer(False, g_sum)
    h_old = call(half_h_body, like(k, half, dtype=BF16), (h,))
    for bit in range(1, term_bits - 1):
        n_keep = call(add_body, like(k, half), (n_keep, n_got))
        n_got = over_term(n_keep, bit)
    n_sum = call(code_sum_body, like(k + TABLE, half, dtype=jnp.int16), (n_keep, n_got))
    n_far = over_term(n_sum, term_bits - 1)
    g_mine = call(round_add_body, like(pk, k, dtype=BF16), (g_sum, g_far))
    g_other = over_term(g_mine, 0)
    h_own = call(new_h_body, like(k, half, dtype=BF16), (n_sum, n_far, g_mine, g_other, h_old))
    h_other = over_term(h_own, 0)

    part = call(first_w_body, like(terms, k), (masked_own, h_own), flops=flops, moved=moved)
    size = terms // 4
    payload = lambda rows: like(rows + TABLE, k, dtype=jnp.int16)
    costs = dict(flops=flops // 4, moved=moved // 4)
    got = {}
    for away in (3, 1, 2):
        body = functools.partial(send_body, away=away)
        sent = call(body, payload(size), (masked_other, part, h_other), **costs)
        got[away] = over_doc(sent, away)
    gram = call(gram_h_body, like(pk, k), (h_other, h_own), **costs)
    keep = call(keep_rows_body, like(size, k), (masked_other, part, h_other), **costs)
    new_h = call(new_h_out_body, like(k, docs, dtype=BF16), (h_other, h_own))
    args = (keep, got[1], got[2], got[3])
    for bit in range(2, bits):
        last = bit == bits - 1
        rows = size if last else size // 2
        outs = (payload(rows),) if last else (payload(rows), like(rows, k))
        sent, *kept = call(functools.partial(next_step_body, bit=bit, last=last), outs, args)
        arrived = over_doc(sent, 1 << bit)
        size, args = rows, (*kept, arrived)
    start = quad_index() * (terms // 4)
    for bit in range(2, bits - 1):
        start += doc_bit(bit) * (terms // 4 >> (bit - 1))
    old = lax.dynamic_slice_in_dim(w, start, size, 0)

    for bit in range(2, bits):
        gram_got = over_doc(gram, 1 << bit)
        gram = call(add_body, like(pk, k), (gram, gram_got))
    grams = {}
    for away in (3, 1, 2):
        grams[away] = over_doc(gram, away)
    g_mine = call(gram_quad_body, like(pk, k, dtype=BF16), (gram, grams[1], grams[2], grams[3]))
    g_other = over_term(g_mine, 0)
    share = call(new_w_body, like(size, k, dtype=BF16), (g_mine, g_other, old, sent, arrived))
    for bit in reversed(range(2, bits - 1)):
        share = join(doc_bit(bit), share, over_doc(share, 1 << bit))
    shares = {away: over_doc(share, away) for away in (3, 1, 2)}
    new_w = call(new_w_out_body, like(terms, k, dtype=BF16), (share, shares[1], shares[2], shares[3]))
    return new_w, new_h


def solution(mesh):
    sizes = dict(mesh.shape)
    return jax.shard_map(
        functools.partial(on_device, n_doc=sizes["doc"], n_term=sizes["term"]),
        mesh=mesh,
        in_specs=(P("term", "doc"), P("term", "doc"), P("term", None), P(None, "doc")),
        out_specs=(P("term", None), P(None, "doc")),
        check_vma=False,
    )
```

```python
import functools

import jax
import jax.numpy as jnp
from jax import lax
from jax.experimental import pallas as pl
from jax.experimental.pallas import tpu as pltpu
from jax.sharding import PartitionSpec as P


BLOCK = 128
F32 = jnp.float32
BF16 = jnp.bfloat16
VMEM = pl.BlockSpec(memory_space=pltpu.VMEM)
HBM = pl.BlockSpec(memory_space=pltpu.HBM)
PIECES = 4
TABLE = 16


def nt(a, b):
    return lax.dot_general(a, b, (((1,), (1,)), ((), ())), preferred_element_type=F32)


def nn(a, b):
    return lax.dot_general(a, b, (((1,), (0,)), ((), ())), preferred_element_type=F32)


def call(body, out, args, hbm=(), scratch=(), flops=1 << 20, moved=1 << 20, limit=24 << 20):
    return pl.pallas_call(
        body,
        out_shape=out,
        in_specs=[HBM if i in hbm else VMEM for i in range(len(args))],
        out_specs=jax.tree.map(lambda _: VMEM, out),
        scratch_shapes=list(scratch),
        compiler_params=pltpu.CompilerParams(vmem_limit_bytes=limit),
        cost_estimate=pl.CostEstimate(flops=flops, bytes_accessed=moved, transcendentals=0),
    )(*args)


def like(*shape, dtype=F32):
    return jax.ShapeDtypeStruct(shape, dtype)


LEVELS = 65534
PER_OCTAVE = 512
EMPTY = -32768


def limits(low, high):
    empty = high == EMPTY
    least = jnp.where(empty, 0.0, jnp.exp2(low * (1.0 / PER_OCTAVE)))
    step = jnp.where(empty, 0.0, (jnp.exp2(high * (1.0 / PER_OCTAVE)) - least) * (1.0 / LEVELS))
    return least, step


def encode(x):
    least = jnp.min(x, axis=0, keepdims=True)
    most = jnp.max(x, axis=0, keepdims=True)
    octave = lambda v: jnp.log2(jnp.maximum(v, 1e-18)) * PER_OCTAVE
    empty = most <= 0.0
    low = jnp.where(empty, EMPTY, jnp.floor(octave(least) - 0.5)).astype(F32)
    high = jnp.where(empty, EMPTY, jnp.ceil(octave(most) + 0.5)).astype(F32)
    base, step = limits(low, high)
    scale = jnp.where(empty, 0.0, 1.0 / jnp.where(empty, 1.0, step))
    code = jnp.clip((x - base) * scale + 0.5, 0.0, LEVELS).astype(jnp.int32) - LEVELS // 2
    return code, low, high


def decode(code, low, high):
    base, step = limits(low, high)
    return base + (code.astype(jnp.int32) + LEVELS // 2).astype(F32) * step


def put_codes(ref, first, groups):
    table = []
    for x in groups:
        code, low, high = encode(x)
        ref[first : first + x.shape[0], :] = code.astype(jnp.int16)
        table += [low, high]
        first += x.shape[0]
    return table


def put_table(ref, at, table):
    row = lax.broadcasted_iota(jnp.int32, (TABLE, table[0].shape[1]), 0)
    out = jnp.zeros(row.shape, F32)
    for i, line in enumerate(table):
        out = jnp.where(row == i, line, out)
    ref[at : at + TABLE, :] = out.astype(jnp.int32).astype(jnp.int16)


def get_table(ref, at):
    return ref[at : at + TABLE, :].astype(jnp.int32).astype(F32)


def get_codes(ref, first, rows, group, table, entry):
    out = []
    for i in range(rows // group):
        low, high = table[entry : entry + 1, :], table[entry + 1 : entry + 2, :]
        out.append(decode(ref[first + i * group : first + (i + 1) * group, :], low, high))
        entry += 2
    return jnp.concatenate(out, axis=0)


def put_parts(ref, parts):
    groups = []
    for x in parts:
        group = min(BLOCK, x.shape[0])
        groups += [x[i : i + group] for i in range(0, x.shape[0], group)]
    table = put_codes(ref, 0, groups)
    put_table(ref, sum(x.shape[0] for x in parts), table)


def get_parts(ref, sizes):
    table = get_table(ref, sum(sizes))
    out, first, entry = [], 0, 0
    for rows in sizes:
        group = min(BLOCK, rows)
        out.append(get_codes(ref, first, rows, group, table, entry))
        first += rows
        entry += 2 * (rows // group)
    return out


def core_index():
    return lax.axis_index("term") & 1


def term_bit(bit):
    return (lax.axis_index("term") >> bit) & 1


def quad_index():
    return lax.axis_index("doc") & 3


def doc_bit(bit):
    return (lax.axis_index("doc") >> bit) & 1


def pack(gram, core):
    k = gram.shape[0]
    h, q = k // 2, k // 4
    e = q // 2
    if core == 0:
        diag, off = gram[:h, :h], gram[:q, h:]
    else:
        diag, off = gram[h:, h:], gram[q:h, h:]
    top = jnp.concatenate([diag[:q], diag[q:]], axis=1)
    low = jnp.concatenate([off[:e], off[e:]], axis=1)
    return jnp.concatenate([top, low], axis=0)


def unpack(one, two):
    k = one.shape[1]
    h, q = k // 2, k // 4
    e = q // 2

    def parts(p):
        diag = jnp.concatenate([p[:q, :h], p[:q, h:]], axis=0)
        off = jnp.concatenate([p[q : q + e, :h], p[q : q + e, h:]], axis=0)
        return diag, off

    diag_one, off_one = parts(one)
    diag_two, off_two = parts(two)
    off = jnp.concatenate([off_one, off_two], axis=0)
    upper = jnp.concatenate([diag_one, off], axis=1)
    lower = jnp.concatenate([off.T, diag_two], axis=1)
    return jnp.concatenate([upper, lower], axis=0)


def pick(core, one, two):
    return jnp.where(core == 0, one, two)


def mask_rows(pattern, half, cols):
    blocks = cols // BLOCK
    lane = lax.broadcasted_iota(jnp.int32, (pattern.shape[0], cols), 1) // BLOCK
    mask = jnp.zeros((pattern.shape[0], cols), F32)
    for c in range(blocks):
        column = pick(half, pattern[:, c : c + 1], pattern[:, blocks + c : blocks + c + 1])
        mask = jnp.where(lane == c, column.astype(F32), mask)
    return mask


def masked_piece(tile_ref, mask, piece, rows):
    out = []
    for r in range(rows // BLOCK):
        first = piece * rows + r * BLOCK
        line = mask[first // BLOCK : first // BLOCK + 1, :].astype(BF16)
        out.append(tile_ref[first : first + BLOCK, :] * line)
    return jnp.concatenate(out, axis=0)


def gram_w_body(w, wt, send, keep):
    core = core_index()
    flipped = w[...].T
    wt[...] = flipped
    gram = nn(flipped, w[...])
    one, two = pack(gram, 0), pack(gram, 1)
    send[...] = pick(core, two, one)
    keep[...] = pick(core, one, two)


def half_h_body(h, out):
    cols = out.shape[1]
    out[...] = h[:, pl.ds(pl.multiple_of(core_index() * cols, cols), cols)]


def numer_body(m, pattern, wt, *refs, other):
    out, masked = refs[-2:]
    side = 1 - core_index() if other else core_index()
    terms, cols = masked.shape
    rows = terms // PIECES
    half = m.at[:, pl.ds(pl.multiple_of(side * cols, cols), cols)]
    mask = mask_rows(pattern[...], side, cols)
    for i in range(PIECES):
        part = slice(i * rows, (i + 1) * rows)
        tile = masked_piece(half, mask, i, rows)
        masked[part, :] = tile
        product = nn(wt[:, part], tile)
        if i == 0:
            out[...] = product
        else:
            out[...] += product


def add_body(a, b, out):
    out[...] = a[...] + b[...]


def round_add_body(a, b, out):
    out[...] = (a[...] + b[...]).astype(BF16)


def code_sum_body(a, b, out):
    total = a[...] + b[...]
    put_table(out, total.shape[0], put_codes(out, 0, [total]))


def new_h_body(mine, other, gram_mine, gram_other, h, out):
    core = core_index()
    a, b = gram_mine[...], gram_other[...]
    gram = unpack(pick(core, a, b), pick(core, b, a))
    old = h[...]
    rows = h.shape[0]
    total = None
    for ref in (mine, other):
        part = get_codes(ref, 0, rows, rows, get_table(ref, rows), 0)
        total = part if total is None else total + part
    out[...] = (old.astype(F32) * total / nn(gram, old)).astype(BF16)


def first_w_body(masked, h, out):
    step = masked.shape[0] // 2
    for r in range(2):
        part = slice(r * step, (r + 1) * step)
        out[part, :] = nt(masked[part, :], h[...])


def piece_of(masked, part, h, index, size):
    start = pl.multiple_of(index * size, size)
    return part[pl.ds(start, size), :] + nt(masked[pl.ds(start, size), :], h[...])


def send_body(masked, part, h, out, *, away):
    put_parts(out, [piece_of(masked, part, h, quad_index() ^ away, masked.shape[0] // 4)])


def keep_rows_body(masked, part, h, out):
    out[...] = piece_of(masked, part, h, quad_index(), out.shape[0])


def gram_h_body(h, h_own, out, *, side_bit):
    gram = nt(h[...], h[...]) + nt(h_own[...], h_own[...])
    part = pick(core_index(), pack(gram, 0), pack(gram, 1))
    rows = out.shape[0]
    out[...] = pick(term_bit(side_bit), part[:rows], part[rows:])


def join_body(mine, other, out, *, side_bit):
    rows = mine.shape[0]
    a, b = mine[...], other[...]
    side = term_bit(side_bit)
    out[:rows, :] = pick(side, a, b)
    out[rows:, :] = pick(side, b, a)


def gram_quad_body(own, one, two, three, out):
    out[...] = ((own[...] + one[...]) + (two[...] + three[...])).astype(BF16)


def new_h_out_body(h, h_own, out):
    core, cols = core_index(), h.shape[1]
    out[:, pl.ds(pl.multiple_of((1 - core) * cols, cols), cols)] = h[...]
    out[:, pl.ds(pl.multiple_of(core * cols, cols), cols)] = h_own[...]


def next_step_body(keep, *refs, bit, last):
    size = keep.shape[0]
    outs = refs[-1:] if last else refs[-2:]
    got = [get_parts(ref, (size,))[0] for ref in refs[: len(refs) - len(outs)]]
    rows = keep[...] + got[0]
    if len(got) > 1:
        rows += got[1] + got[2]
    if last:
        put_parts(outs[0], [rows])
        return
    half = size // 2
    low, high = rows[:half], rows[half:]
    side = doc_bit(bit)
    put_parts(outs[0], [pick(side, high, low)])
    outs[1][...] = pick(side, low, high)


def total_body(sent, got, out):
    size = sent.shape[0] - TABLE
    put_parts(out.at[0], [get_parts(sent, (size,))[0] + get_parts(got, (size,))[0]])


def new_w_body(gram_mine, gram_other, w, own, one, two, three, out):
    core = core_index()
    a, b = gram_mine[...], gram_other[...]
    gram = unpack(pick(core, a, b), pick(core, b, a))
    pieces, size = own.shape[0], own.shape[1] - TABLE
    for away, ref in enumerate((own, one, two, three)):
        for i in range(pieces):
            start = pl.multiple_of(((quad_index() ^ away) * pieces + i) * size, size)
            old = w[pl.ds(start, size), :]
            total = get_parts(ref.at[i], (size,))[0]
            out[pl.ds(start, size), :] = (old.astype(F32) * total / nn(old, gram)).astype(BF16)


def swap(x, axis, size, away):
    return lax.ppermute(x, axis, [(i, i ^ away) for i in range(size)])


def join(bit, mine, other):
    return jnp.concatenate([jnp.where(bit == 0, mine, other), jnp.where(bit == 0, other, mine)], axis=0)


def on_device(m, pattern, w, h, *, n_doc, n_term):
    return update(m, pattern, w, h, n_doc, n_term)


def update(m, pattern, w, h, n_doc, n_term):
    terms, docs = m.shape
    k = w.shape[1]
    half = docs // 2
    pk = 3 * k // 8
    bits = n_doc.bit_length() - 1
    term_bits = n_term.bit_length() - 1

    def over_term(x, bit):
        return swap(x, "term", n_term, 1 << bit)

    def over_doc(x, away):
        return swap(x, "doc", n_doc, away)

    flops = terms * docs * k
    moved = 2 * terms * docs

    side = like(terms, half, dtype=BF16)
    wt, g_send, g_keep = call(
        gram_w_body, (like(k, terms, dtype=BF16), like(pk, k), like(pk, k)), (w,), flops=32 * flops, moved=moved
    )
    g_got = over_term(g_send, 0)

    def numer(is_other, *after):
        body = functools.partial(numer_body, other=is_other)
        return call(body, (like(k, half), side), (m, pattern, wt, *after), flops=flops, moved=moved)

    n_send, masked_other = numer(True)
    n_got = over_term(n_send, 0)
    for bit in range(1, term_bits - 1):
        g_keep = call(add_body, like(pk, k), (g_keep, g_got))
        g_got = over_term(g_keep, bit)
    g_sum = call(add_body, like(pk, k), (g_keep, g_got))
    g_far = over_term(g_sum, term_bits - 1)
    n_keep, masked_own = numer(False, g_sum)
    h_old = call(half_h_body, like(k, half, dtype=BF16), (h,))
    for bit in range(1, term_bits - 1):
        n_keep = call(add_body, like(k, half), (n_keep, n_got))
        n_got = over_term(n_keep, bit)
    n_sum = call(code_sum_body, like(k + TABLE, half, dtype=jnp.int16), (n_keep, n_got))
    n_far = over_term(n_sum, term_bits - 1)
    g_mine = call(round_add_body, like(pk, k, dtype=BF16), (g_sum, g_far))
    g_other = over_term(g_mine, 0)
    h_own = call(new_h_body, like(k, half, dtype=BF16), (n_sum, n_far, g_mine, g_other, h_old))
    h_other = over_term(h_own, 0)

    part = call(first_w_body, like(terms, k), (masked_own, h_own), flops=flops, moved=moved)
    size = terms // 4
    payload = lambda rows: like(rows + TABLE, k, dtype=jnp.int16)
    costs = dict(flops=flops // 4, moved=moved // 4)
    got = {}
    for away in (3, 1, 2):
        body = functools.partial(send_body, away=away)
        sent = call(body, payload(size), (masked_other, part, h_other), **costs)
        got[away] = over_doc(sent, away)
    body = functools.partial(gram_h_body, side_bit=term_bits - 1)
    gram = call(body, like(pk // 2, k), (h_other, h_own), **costs)
    keep = call(keep_rows_body, like(size, k), (masked_other, part, h_other), **costs)
    new_h = call(new_h_out_body, like(k, docs, dtype=BF16), (h_other, h_own))
    args = (keep, got[1], got[2], got[3])
    for bit in range(2, bits):
        last = bit == bits - 1
        rows = size if last else size // 2
        outs = (payload(rows),) if last else (payload(rows), like(rows, k))
        sent, *kept = call(functools.partial(next_step_body, bit=bit, last=last), outs, args)
        arrived = over_doc(sent, 1 << bit)
        size, args = rows, (*kept, arrived)
    share = call(total_body, like(1, size + TABLE, k, dtype=jnp.int16), (sent, arrived))
    for bit in reversed(range(2, bits - 1)):
        share = join(doc_bit(bit), share, over_doc(share, 1 << bit))
    shares = {}
    for away in (3, 1, 2):
        shares[away] = over_doc(share, away)

    for bit in range(2, bits):
        gram_got = over_doc(gram, 1 << bit)
        gram = call(add_body, like(pk // 2, k), (gram, gram_got))
    grams = {}
    for away in (3, 1, 2):
        grams[away] = over_doc(gram, away)
    g_half = call(gram_quad_body, like(pk // 2, k, dtype=BF16), (gram, grams[1], grams[2], grams[3]))
    g_far = over_term(g_half, term_bits - 1)
    body = functools.partial(join_body, side_bit=term_bits - 1)
    g_mine = call(body, like(pk, k, dtype=BF16), (g_half, g_far))
    g_other = over_term(g_mine, 0)
    ends = (share, shares[1], shares[2], shares[3])
    new_w = call(new_w_body, like(terms, k, dtype=BF16), (g_mine, g_other, w, *ends), flops=flops // 4)
    return new_w, new_h


def solution(mesh):
    sizes = dict(mesh.shape)
    return jax.shard_map(
        functools.partial(on_device, n_doc=sizes["doc"], n_term=sizes["term"]),
        mesh=mesh,
        in_specs=(P("term", "doc"), P("term", "doc"), P("term", None), P(None, "doc")),
        out_specs=(P("term", None), P(None, "doc")),
        check_vma=False,
    )
```

```python
import functools

import jax
import jax.numpy as jnp
from jax import lax
from jax.experimental import pallas as pl
from jax.experimental.pallas import tpu as pltpu
from jax.sharding import PartitionSpec as P


BLOCK = 128
F32 = jnp.float32
BF16 = jnp.bfloat16
VMEM = pl.BlockSpec(memory_space=pltpu.VMEM)
HBM = pl.BlockSpec(memory_space=pltpu.HBM)
PIECES = 4
TABLE = 8


def nt(a, b):
    return lax.dot_general(a, b, (((1,), (1,)), ((), ())), preferred_element_type=F32)


def nn(a, b):
    return lax.dot_general(a, b, (((1,), (0,)), ((), ())), preferred_element_type=F32)


def call(body, out, args, spec=None, scratch=(), flops=1 << 20, moved=1 << 20, limit=24 << 20):
    return pl.pallas_call(
        body,
        out_shape=out,
        in_specs=[VMEM] * len(args),
        out_specs=jax.tree.map(lambda _: spec or VMEM, out),
        scratch_shapes=list(scratch),
        compiler_params=pltpu.CompilerParams(vmem_limit_bytes=limit),
        cost_estimate=pl.CostEstimate(flops=flops, bytes_accessed=moved, transcendentals=0),
    )(*args)


def like(*shape, dtype=F32):
    return jax.ShapeDtypeStruct(shape, dtype)


LEVELS = 65534
PER_OCTAVE = 512
EMPTY = -32768


def limits(low, high):
    empty = high == EMPTY
    least = jnp.where(empty, 0.0, jnp.exp2(low * (1.0 / PER_OCTAVE)))
    step = jnp.where(empty, 0.0, (jnp.exp2(high * (1.0 / PER_OCTAVE)) - least) * (1.0 / LEVELS))
    return least, step


def encode(x):
    least = jnp.min(x, axis=0, keepdims=True)
    most = jnp.max(x, axis=0, keepdims=True)
    octave = lambda v: jnp.log2(jnp.maximum(v, 1e-18)) * PER_OCTAVE
    empty = most <= 0.0
    low = jnp.where(empty, EMPTY, jnp.floor(octave(least) - 0.5)).astype(F32)
    high = jnp.where(empty, EMPTY, jnp.ceil(octave(most) + 0.5)).astype(F32)
    base, step = limits(low, high)
    scale = jnp.where(empty, 0.0, 1.0 / jnp.where(empty, 1.0, step))
    code = jnp.clip((x - base) * scale + 0.5, 0.0, LEVELS).astype(jnp.int32) - LEVELS // 2
    return code, low, high


def decode(code, low, high):
    base, step = limits(low, high)
    return base + (code.astype(jnp.int32) + LEVELS // 2).astype(F32) * step


def put_codes(ref, first, groups):
    table = []
    for x in groups:
        code, low, high = encode(x)
        ref[first : first + x.shape[0], :] = code.astype(jnp.int16)
        table += [low, high]
        first += x.shape[0]
    return table


def put_table(ref, at, table):
    row = lax.broadcasted_iota(jnp.int32, (TABLE, table[0].shape[1]), 0)
    out = jnp.zeros(row.shape, F32)
    for i, line in enumerate(table):
        out = jnp.where(row == i, line, out)
    ref[at : at + TABLE, :] = out.astype(jnp.int32).astype(jnp.int16)


def get_table(ref, at):
    return ref[at : at + TABLE, :].astype(jnp.int32).astype(F32)


def get_codes(ref, first, rows, group, table, entry):
    out = []
    for i in range(rows // group):
        low, high = table[entry : entry + 1, :], table[entry + 1 : entry + 2, :]
        out.append(decode(ref[first + i * group : first + (i + 1) * group, :], low, high))
        entry += 2
    return jnp.concatenate(out, axis=0)


def put_parts(ref, parts):
    groups = []
    for x in parts:
        group = min(BLOCK, x.shape[0])
        groups += [x[i : i + group] for i in range(0, x.shape[0], group)]
    table = put_codes(ref, 0, groups)
    put_table(ref, sum(x.shape[0] for x in parts), table)


def get_parts(ref, sizes):
    table = get_table(ref, sum(sizes))
    out, first, entry = [], 0, 0
    for rows in sizes:
        group = min(BLOCK, rows)
        out.append(get_codes(ref, first, rows, group, table, entry))
        first += rows
        entry += 2 * (rows // group)
    return out


def core_index():
    return lax.axis_index("term") & 1


def term_bit(bit):
    return (lax.axis_index("term") >> bit) & 1


def quad_index():
    return lax.axis_index("doc") & 3


def doc_bit(bit):
    return (lax.axis_index("doc") >> bit) & 1


def pack(gram, core):
    k = gram.shape[0]
    h, q = k // 2, k // 4
    e = q // 2
    if core == 0:
        diag, off = gram[:h, :h], gram[:q, h:]
    else:
        diag, off = gram[h:, h:], gram[q:h, h:]
    top = jnp.concatenate([diag[:q], diag[q:]], axis=1)
    low = jnp.concatenate([off[:e], off[e:]], axis=1)
    return jnp.concatenate([top, low], axis=0)


def unpack(one, two):
    k = one.shape[1]
    h, q = k // 2, k // 4
    e = q // 2

    def parts(p):
        diag = jnp.concatenate([p[:q, :h], p[:q, h:]], axis=0)
        off = jnp.concatenate([p[q : q + e, :h], p[q : q + e, h:]], axis=0)
        return diag, off

    diag_one, off_one = parts(one)
    diag_two, off_two = parts(two)
    off = jnp.concatenate([off_one, off_two], axis=0)
    upper = jnp.concatenate([diag_one, off], axis=1)
    lower = jnp.concatenate([off.T, diag_two], axis=1)
    return jnp.concatenate([upper, lower], axis=0)


def pick(core, one, two):
    return jnp.where(core == 0, one, two)


def mask_rows(pattern, half, cols):
    blocks = cols // BLOCK
    lane = lax.broadcasted_iota(jnp.int32, (pattern.shape[0], cols), 1) // BLOCK
    mask = jnp.zeros((pattern.shape[0], cols), F32)
    for c in range(blocks):
        column = pick(half, pattern[:, c : c + 1], pattern[:, blocks + c : blocks + c + 1])
        mask = jnp.where(lane == c, column.astype(F32), mask)
    return mask


def masked_piece(tile_ref, mask, piece, rows):
    out = []
    for r in range(rows // BLOCK):
        first = piece * rows + r * BLOCK
        line = mask[first // BLOCK : first // BLOCK + 1, :].astype(BF16)
        out.append(tile_ref[first : first + BLOCK, :] * line)
    return jnp.concatenate(out, axis=0)


def gram_w_body(w, wt, send, keep):
    core = core_index()
    flipped = w[...].T
    wt[...] = flipped
    gram = nn(flipped, w[...])
    one, two = pack(gram, 0), pack(gram, 1)
    send[...] = pick(core, two, one)
    keep[...] = pick(core, one, two)


def half_h_body(h, out):
    cols = out.shape[1]
    out[...] = h[:, pl.ds(pl.multiple_of(core_index() * cols, cols), cols)]


def numer_body(m, pattern, wt, *refs, other):
    out, masked = refs[-2:]
    side = 1 - core_index() if other else core_index()
    terms, cols = masked.shape
    rows = terms // PIECES
    half = m.at[:, pl.ds(pl.multiple_of(side * cols, cols), cols)]
    mask = mask_rows(pattern[...], side, cols)
    for i in range(PIECES):
        part = slice(i * rows, (i + 1) * rows)
        tile = masked_piece(half, mask, i, rows)
        masked[part, :] = tile
        product = nn(wt[:, part], tile)
        if i == 0:
            out[...] = product
        else:
            out[...] += product


def add_body(a, b, out):
    out[...] = a[...] + b[...]


def round_add_body(a, b, out):
    out[...] = (a[...] + b[...]).astype(BF16)


def code_sum_body(a, b, out):
    total = a[...] + b[...]
    put_table(out, total.shape[0], put_codes(out, 0, [total]))


def new_h_body(mine, other, gram_mine, gram_other, h, out):
    core = core_index()
    a, b = gram_mine[...], gram_other[...]
    gram = unpack(pick(core, a, b), pick(core, b, a))
    old = h[...]
    rows = h.shape[0]
    total = None
    for ref in (mine, other):
        part = get_codes(ref, 0, rows, rows, get_table(ref, rows), 0)
        total = part if total is None else total + part
    out[...] = (old.astype(F32) * total / nn(gram, old)).astype(BF16)


def first_w_body(masked, h, out):
    step = masked.shape[0] // 2
    for r in range(2):
        part = slice(r * step, (r + 1) * step)
        out[part, :] = nt(masked[part, :], h[...])


def piece_of(masked, part, h, index, size):
    start = pl.multiple_of(index * size, size)
    return part[pl.ds(start, size), :] + nt(masked[pl.ds(start, size), :], h[...])


def send_body(masked, part, h, out, *, away):
    put_parts(out, [piece_of(masked, part, h, quad_index() ^ away, masked.shape[0] // 4)])


def keep_rows_body(masked, part, h, out):
    out[...] = piece_of(masked, part, h, quad_index(), out.shape[0])


def gram_h_body(h, h_own, out, *, side_bit):
    gram = nt(h[...], h[...]) + nt(h_own[...], h_own[...])
    part = pick(core_index(), pack(gram, 0), pack(gram, 1))
    rows = out.shape[0]
    out[...] = pick(term_bit(side_bit), part[:rows], part[rows:])


def join_body(mine, other, out, *, side_bit):
    rows = mine.shape[0]
    a, b = mine[...], other[...]
    side = term_bit(side_bit)
    out[:rows, :] = pick(side, a, b)
    out[rows:, :] = pick(side, b, a)


def gram_quad_body(own, one, two, three, out):
    out[...] = ((own[...] + one[...]) + (two[...] + three[...])).astype(BF16)


def new_h_out_body(h, h_own, out):
    core, cols = core_index(), h.shape[1]
    out[:, pl.ds(pl.multiple_of((1 - core) * cols, cols), cols)] = h[...]
    out[:, pl.ds(pl.multiple_of(core * cols, cols), cols)] = h_own[...]


def next_step_body(keep, *refs, bit, last):
    size = keep.shape[0]
    outs = refs[-1:] if last else refs[-2:]
    got = [get_parts(ref, (size,))[0] for ref in refs[: len(refs) - len(outs)]]
    rows = keep[...] + got[0]
    if len(got) > 1:
        rows += got[1] + got[2]
    if last:
        put_parts(outs[0], [rows])
        return
    half = size // 2
    low, high = rows[:half], rows[half:]
    side = doc_bit(bit)
    put_parts(outs[0], [pick(side, high, low)])
    outs[1][...] = pick(side, low, high)


def total_body(sent, got, out):
    size = sent.shape[0] - TABLE
    put_parts(out.at[0], [get_parts(sent, (size,))[0] + get_parts(got, (size,))[0]])


def ratio_body(gram_mine, gram_other, w, out):
    core = core_index()
    a, b = gram_mine[...], gram_other[...]
    gram = unpack(pick(core, a, b), pick(core, b, a))
    old = w[...]
    out[...] = old.astype(F32) / nn(old, gram)


def new_w_body(ratio, own, one, two, three, out, held, sems):
    pieces, size = own.shape[0], own.shape[1] - TABLE
    copies = []
    for away, ref in enumerate((own, one, two, three)):
        first = (quad_index() ^ away) * pieces
        for i in range(pieces):
            rows = pl.ds(pl.multiple_of((first + i) * size, size), size)
            held[rows, :] = (ratio[rows, :] * get_parts(ref.at[i], (size,))[0]).astype(BF16)
        rows = pl.ds(pl.multiple_of(first * size, pieces * size), pieces * size)
        copies.append(pltpu.make_async_copy(held.at[rows, :], out.at[rows, :], sems.at[away]))
        copies[-1].start()
    for copy in copies:
        copy.wait()


def swap(x, axis, size, away):
    return lax.ppermute(x, axis, [(i, i ^ away) for i in range(size)])


def join(bit, mine, other):
    return jnp.concatenate([jnp.where(bit == 0, mine, other), jnp.where(bit == 0, other, mine)], axis=0)


def on_device(m, pattern, w, h, *, n_doc, n_term):
    return update(m, pattern, w, h, n_doc, n_term)


def update(m, pattern, w, h, n_doc, n_term):
    terms, docs = m.shape
    k = w.shape[1]
    half = docs // 2
    pk = 3 * k // 8
    bits = n_doc.bit_length() - 1
    term_bits = n_term.bit_length() - 1

    def over_term(x, bit):
        return swap(x, "term", n_term, 1 << bit)

    def over_doc(x, away):
        return swap(x, "doc", n_doc, away)

    flops = terms * docs * k
    moved = 2 * terms * docs

    side = like(terms, half, dtype=BF16)
    wt, g_send, g_keep = call(
        gram_w_body, (like(k, terms, dtype=BF16), like(pk, k), like(pk, k)), (w,), flops=32 * flops, moved=moved
    )
    g_got = over_term(g_send, 0)

    def numer(is_other, *after):
        body = functools.partial(numer_body, other=is_other)
        return call(body, (like(k, half), side), (m, pattern, wt, *after), flops=flops, moved=moved)

    n_send, masked_other = numer(True)
    n_got = over_term(n_send, 0)
    for bit in range(1, term_bits - 1):
        g_keep = call(add_body, like(pk, k), (g_keep, g_got))
        g_got = over_term(g_keep, bit)
    g_sum = call(add_body, like(pk, k), (g_keep, g_got))
    g_far = over_term(g_sum, term_bits - 1)
    n_keep, masked_own = numer(False, g_sum)
    h_old = call(half_h_body, like(k, half, dtype=BF16), (h,))
    for bit in range(1, term_bits - 1):
        n_keep = call(add_body, like(k, half), (n_keep, n_got))
        n_got = over_term(n_keep, bit)
    n_sum = call(code_sum_body, like(k + TABLE, half, dtype=jnp.int16), (n_keep, n_got))
    n_far = over_term(n_sum, term_bits - 1)
    g_mine = call(round_add_body, like(pk, k, dtype=BF16), (g_sum, g_far))
    g_other = over_term(g_mine, 0)
    h_own = call(new_h_body, like(k, half, dtype=BF16), (n_sum, n_far, g_mine, g_other, h_old))
    h_other = over_term(h_own, 0)

    part = call(first_w_body, like(terms, k), (masked_own, h_own), flops=flops, moved=moved)
    size = terms // 4
    payload = lambda rows: like(rows + TABLE, k, dtype=jnp.int16)
    costs = dict(flops=flops // 4, moved=moved // 4)
    got = {}
    for away in (3, 1, 2):
        body = functools.partial(send_body, away=away)
        sent = call(body, payload(size), (masked_other, part, h_other), **costs)
        got[away] = over_doc(sent, away)
    body = functools.partial(gram_h_body, side_bit=term_bits - 1)
    gram = call(body, like(pk // 2, k), (h_other, h_own), **costs)
    keep = call(keep_rows_body, like(size, k), (masked_other, part, h_other), **costs)
    new_h = call(new_h_out_body, like(k, docs, dtype=BF16), (h_other, h_own))
    args = (keep, got[1], got[2], got[3])
    for bit in range(2, bits):
        last = bit == bits - 1
        rows = size if last else size // 2
        outs = (payload(rows),) if last else (payload(rows), like(rows, k))
        sent, *kept = call(functools.partial(next_step_body, bit=bit, last=last), outs, args)
        arrived = over_doc(sent, 1 << bit)
        size, args = rows, (*kept, arrived)
    share = call(total_body, like(1, size + TABLE, k, dtype=jnp.int16), (sent, arrived))
    for bit in reversed(range(2, bits - 1)):
        share = join(doc_bit(bit), share, over_doc(share, 1 << bit))
    shares = {}
    for away in (3, 1, 2):
        shares[away] = over_doc(share, away)

    for bit in range(2, bits):
        gram_got = over_doc(gram, 1 << bit)
        gram = call(add_body, like(pk // 2, k), (gram, gram_got))
    grams = {}
    for away in (3, 1, 2):
        grams[away] = over_doc(gram, away)
    g_half = call(gram_quad_body, like(pk // 2, k, dtype=BF16), (gram, grams[1], grams[2], grams[3]))
    g_far = over_term(g_half, term_bits - 1)
    body = functools.partial(join_body, side_bit=term_bits - 1)
    g_mine = call(body, like(pk, k, dtype=BF16), (g_half, g_far))
    g_other = over_term(g_mine, 0)
    ratio = call(ratio_body, like(terms, k), (g_mine, g_other, w), flops=flops // 4)
    new_w = call(
        new_w_body,
        like(terms, k, dtype=BF16),
        (ratio, share, shares[1], shares[2], shares[3]),
        spec=HBM,
        scratch=(pltpu.VMEM((terms, k), BF16), pltpu.SemaphoreType.DMA((4,))),
    )
    return new_w, new_h


def solution(mesh):
    sizes = dict(mesh.shape)
    return jax.shard_map(
        functools.partial(on_device, n_doc=sizes["doc"], n_term=sizes["term"]),
        mesh=mesh,
        in_specs=(P("term", "doc"), P("term", "doc"), P("term", None), P(None, "doc")),
        out_specs=(P("term", None), P(None, "doc")),
        check_vma=False,
    )
```

```python
import functools

import jax
import jax.numpy as jnp
from jax import lax
from jax.experimental import pallas as pl
from jax.experimental.pallas import tpu as pltpu
from jax.sharding import PartitionSpec as P


BLOCK = 128
F32 = jnp.float32
BF16 = jnp.bfloat16
VMEM = pl.BlockSpec(memory_space=pltpu.VMEM)
HBM = pl.BlockSpec(memory_space=pltpu.HBM)
PIECES = 2
TABLE = 8


def nt(a, b):
    return lax.dot_general(a, b, (((1,), (1,)), ((), ())), preferred_element_type=F32)


def nn(a, b):
    return lax.dot_general(a, b, (((1,), (0,)), ((), ())), preferred_element_type=F32)


def call(body, out, args, spec=None, scratch=(), flops=1 << 20, moved=1 << 20, limit=24 << 20):
    return pl.pallas_call(
        body,
        out_shape=out,
        in_specs=[VMEM] * len(args),
        out_specs=jax.tree.map(lambda _: spec or VMEM, out),
        scratch_shapes=list(scratch),
        compiler_params=pltpu.CompilerParams(vmem_limit_bytes=limit),
        cost_estimate=pl.CostEstimate(flops=flops, bytes_accessed=moved, transcendentals=0),
    )(*args)


def like(*shape, dtype=F32):
    return jax.ShapeDtypeStruct(shape, dtype)


LEVELS = 65534
PER_OCTAVE = 512
EMPTY = -32768


def limits(low, high):
    empty = high == EMPTY
    least = jnp.where(empty, 0.0, jnp.exp2(low * (1.0 / PER_OCTAVE)))
    step = jnp.where(empty, 0.0, (jnp.exp2(high * (1.0 / PER_OCTAVE)) - least) * (1.0 / LEVELS))
    return least, step


def encode(x):
    x = x * lax.rsqrt(jnp.maximum(x, 1e-30))
    least = jnp.min(x, axis=0, keepdims=True)
    most = jnp.max(x, axis=0, keepdims=True)
    octave = lambda v: jnp.log2(jnp.maximum(v, 1e-18)) * PER_OCTAVE
    empty = most <= 0.0
    low = jnp.where(empty, EMPTY, jnp.floor(octave(least) - 0.5)).astype(F32)
    high = jnp.where(empty, EMPTY, jnp.ceil(octave(most) + 0.5)).astype(F32)
    base, step = limits(low, high)
    scale = jnp.where(empty, 0.0, 1.0 / jnp.where(empty, 1.0, step))
    code = jnp.clip((x - base) * scale + 0.5, 0.0, LEVELS).astype(jnp.int32) - LEVELS // 2
    return code, low, high


def decode(code, low, high):
    base, step = limits(low, high)
    root = base + (code.astype(jnp.int32) + LEVELS // 2).astype(F32) * step
    return root * root


def put_codes(ref, first, groups):
    table = []
    for x in groups:
        code, low, high = encode(x)
        ref[first : first + x.shape[0], :] = code.astype(jnp.int16)
        table += [low, high]
        first += x.shape[0]
    return table


def put_table(ref, at, table):
    row = lax.broadcasted_iota(jnp.int32, (TABLE, table[0].shape[1]), 0)
    out = jnp.zeros(row.shape, F32)
    for i, line in enumerate(table):
        out = jnp.where(row == i, line, out)
    ref[at : at + TABLE, :] = out.astype(jnp.int32).astype(jnp.int16)


def get_table(ref, at):
    return ref[at : at + TABLE, :].astype(jnp.int32).astype(F32)


def get_codes(ref, first, rows, group, table, entry):
    out = []
    for i in range(rows // group):
        low, high = table[entry : entry + 1, :], table[entry + 1 : entry + 2, :]
        out.append(decode(ref[first + i * group : first + (i + 1) * group, :], low, high))
        entry += 2
    return jnp.concatenate(out, axis=0)


def put_parts(ref, parts):
    groups = []
    for x in parts:
        group = min(BLOCK, x.shape[0])
        groups += [x[i : i + group] for i in range(0, x.shape[0], group)]
    table = put_codes(ref, 0, groups)
    put_table(ref, sum(x.shape[0] for x in parts), table)


def get_parts(ref, sizes):
    table = get_table(ref, sum(sizes))
    out, first, entry = [], 0, 0
    for rows in sizes:
        group = min(BLOCK, rows)
        out.append(get_codes(ref, first, rows, group, table, entry))
        first += rows
        entry += 2 * (rows // group)
    return out


def core_index():
    return lax.axis_index("term") & 1


def term_bit(bit):
    return (lax.axis_index("term") >> bit) & 1


def quad_index():
    return lax.axis_index("doc") & 3


def doc_bit(bit):
    return (lax.axis_index("doc") >> bit) & 1


def pack(gram, core):
    k = gram.shape[0]
    h, q = k // 2, k // 4
    e = q // 2
    if core == 0:
        diag, off = gram[:h, :h], gram[:q, h:]
    else:
        diag, off = gram[h:, h:], gram[q:h, h:]
    top = jnp.concatenate([diag[:q], diag[q:]], axis=1)
    low = jnp.concatenate([off[:e], off[e:]], axis=1)
    return jnp.concatenate([top, low], axis=0)


def unpack(one, two):
    k = one.shape[1]
    h, q = k // 2, k // 4
    e = q // 2

    def parts(p):
        diag = jnp.concatenate([p[:q, :h], p[:q, h:]], axis=0)
        off = jnp.concatenate([p[q : q + e, :h], p[q : q + e, h:]], axis=0)
        return diag, off

    diag_one, off_one = parts(one)
    diag_two, off_two = parts(two)
    off = jnp.concatenate([off_one, off_two], axis=0)
    upper = jnp.concatenate([diag_one, off], axis=1)
    lower = jnp.concatenate([off.T, diag_two], axis=1)
    return jnp.concatenate([upper, lower], axis=0)


def pick(core, one, two):
    return jnp.where(core == 0, one, two)


def mask_rows(pattern, half, cols):
    blocks = cols // BLOCK
    lane = lax.broadcasted_iota(jnp.int32, (pattern.shape[0], cols), 1) // BLOCK
    mask = jnp.zeros((pattern.shape[0], cols), F32)
    for c in range(blocks):
        column = pick(half, pattern[:, c : c + 1], pattern[:, blocks + c : blocks + c + 1])
        mask = jnp.where(lane == c, column.astype(F32), mask)
    return mask


def masked_piece(tile_ref, mask, piece, rows):
    out = []
    for r in range(rows // BLOCK):
        first = piece * rows + r * BLOCK
        line = mask[first // BLOCK : first // BLOCK + 1, :].astype(BF16)
        out.append(tile_ref[first : first + BLOCK, :] * line)
    return jnp.concatenate(out, axis=0)


def gram_w_body(w, wt, send, keep):
    core = core_index()
    flipped = w[...].T
    wt[...] = flipped
    gram = nn(flipped, w[...])
    one, two = pack(gram, 0), pack(gram, 1)
    send[...] = pick(core, two, one)
    keep[...] = pick(core, one, two)


def half_h_body(h, out):
    cols = out.shape[1]
    out[...] = h[:, pl.ds(pl.multiple_of(core_index() * cols, cols), cols)]


def numer_body(m, pattern, wt, *refs, other):
    out, masked = refs[-2:]
    side = 1 - core_index() if other else core_index()
    terms, cols = masked.shape
    rows = terms // PIECES
    half = m.at[:, pl.ds(pl.multiple_of(side * cols, cols), cols)]
    mask = mask_rows(pattern[...], side, cols)
    for i in range(PIECES):
        part = slice(i * rows, (i + 1) * rows)
        tile = masked_piece(half, mask, i, rows)
        masked[part, :] = tile
        product = nn(wt[:, part], tile)
        if i == 0:
            out[...] = product
        else:
            out[...] += product


def add_body(a, b, out):
    out[...] = a[...] + b[...]


def round_add_body(a, b, out):
    out[...] = (a[...] + b[...]).astype(BF16)


def code_sum_body(a, b, out):
    total = a[...] + b[...]
    put_table(out, total.shape[0], put_codes(out, 0, [total]))


def new_h_body(mine, other, gram_mine, gram_other, h, out):
    core = core_index()
    a, b = gram_mine[...], gram_other[...]
    gram = unpack(pick(core, a, b), pick(core, b, a))
    old = h[...]
    rows = h.shape[0]
    total = None
    for ref in (mine, other):
        part = get_codes(ref, 0, rows, rows, get_table(ref, rows), 0)
        total = part if total is None else total + part
    out[...] = (old.astype(F32) * total / nn(gram, old)).astype(BF16)


def first_w_body(masked, h, out):
    step = masked.shape[0] // 2
    for r in range(2):
        part = slice(r * step, (r + 1) * step)
        out[part, :] = nt(masked[part, :], h[...])


def piece_of(masked, part, h, index, size):
    start = pl.multiple_of(index * size, size)
    return part[pl.ds(start, size), :] + nt(masked[pl.ds(start, size), :], h[...])


def send_body(masked, part, h, out, *, away):
    put_parts(out, [piece_of(masked, part, h, quad_index() ^ away, masked.shape[0] // 4)])


def keep_rows_body(masked, part, h, out):
    out[...] = piece_of(masked, part, h, quad_index(), out.shape[0])


def gram_h_body(h, h_own, out, *, side_bit):
    gram = nt(h[...], h[...]) + nt(h_own[...], h_own[...])
    part = pick(core_index(), pack(gram, 0), pack(gram, 1))
    rows = out.shape[0]
    out[...] = pick(term_bit(side_bit), part[:rows], part[rows:])


def gram_quad_body(own, one, two, three, out):
    out[...] = ((own[...] + one[...]) + (two[...] + three[...])).astype(BF16)


def new_h_out_body(h, h_own, out):
    core, cols = core_index(), h.shape[1]
    out[:, pl.ds(pl.multiple_of((1 - core) * cols, cols), cols)] = h[...]
    out[:, pl.ds(pl.multiple_of(core * cols, cols), cols)] = h_own[...]


def next_step_body(keep, *refs, bit, last):
    size = keep.shape[0]
    outs = refs[-1:] if last else refs[-2:]
    got = [get_parts(ref, (size,))[0] for ref in refs[: len(refs) - len(outs)]]
    rows = keep[...] + got[0]
    if len(got) > 1:
        rows += got[1] + got[2]
    if last:
        put_parts(outs[0], [rows])
        return
    half = size // 2
    low, high = rows[:half], rows[half:]
    side = doc_bit(bit)
    put_parts(outs[0], [pick(side, high, low)])
    outs[1][...] = pick(side, low, high)


def total_body(sent, got, out):
    size = sent.shape[0] - TABLE
    put_parts(out.at[0], [get_parts(sent, (size,))[0] + get_parts(got, (size,))[0]])


def ratio_body(here, near, far, across, w, out, *, side_bit):
    core, side = core_index(), term_bit(side_bit)

    def both(one, two):
        return jnp.concatenate([pick(side, one, two), pick(side, two, one)], axis=0)

    mine, other = both(here[...], far[...]), both(near[...], across[...])
    gram = unpack(pick(core, mine, other), pick(core, other, mine))
    old = w[...]
    out[...] = old.astype(F32) / nn(old, gram)


def new_w_body(ratio, own, one, two, three, out, held, sems):
    pieces, size = own.shape[0], own.shape[1] - TABLE
    copies = []
    for away, ref in enumerate((own, one, two, three)):
        first = (quad_index() ^ away) * pieces
        for i in range(pieces):
            rows = pl.ds(pl.multiple_of((first + i) * size, size), size)
            held[rows, :] = (ratio[rows, :] * get_parts(ref.at[i], (size,))[0]).astype(BF16)
        rows = pl.ds(pl.multiple_of(first * size, pieces * size), pieces * size)
        copies.append(pltpu.make_async_copy(held.at[rows, :], out.at[rows, :], sems.at[away]))
        copies[-1].start()
    for copy in copies:
        copy.wait()


def swap(x, axis, size, away):
    return lax.ppermute(x, axis, [(i, i ^ away) for i in range(size)])


def join(bit, mine, other):
    return jnp.concatenate([jnp.where(bit == 0, mine, other), jnp.where(bit == 0, other, mine)], axis=0)


def on_device(m, pattern, w, h, *, n_doc, n_term):
    return update(m, pattern, w, h, n_doc, n_term)


def update(m, pattern, w, h, n_doc, n_term):
    terms, docs = m.shape
    k = w.shape[1]
    half = docs // 2
    pk = 3 * k // 8
    bits = n_doc.bit_length() - 1
    term_bits = n_term.bit_length() - 1

    def over_term(x, bit):
        return swap(x, "term", n_term, 1 << bit)

    def over_doc(x, away):
        return swap(x, "doc", n_doc, away)

    flops = terms * docs * k
    moved = 2 * terms * docs

    side = like(terms, half, dtype=BF16)
    wt, g_send, g_keep = call(
        gram_w_body, (like(k, terms, dtype=BF16), like(pk, k), like(pk, k)), (w,), flops=32 * flops, moved=moved
    )
    g_got = over_term(g_send, 0)

    def numer(is_other, *after):
        body = functools.partial(numer_body, other=is_other)
        return call(body, (like(k, half), side), (m, pattern, wt, *after), flops=flops, moved=moved)

    n_send, masked_other = numer(True)
    n_got = over_term(n_send, 0)
    for bit in range(1, term_bits - 1):
        g_keep = call(add_body, like(pk, k), (g_keep, g_got))
        g_got = over_term(g_keep, bit)
    g_sum = call(add_body, like(pk, k), (g_keep, g_got))
    g_far = over_term(g_sum, term_bits - 1)
    n_keep, masked_own = numer(False, g_sum)
    h_old = call(half_h_body, like(k, half, dtype=BF16), (h,))
    for bit in range(1, term_bits - 1):
        n_keep = call(add_body, like(k, half), (n_keep, n_got))
        n_got = over_term(n_keep, bit)
    n_sum = call(code_sum_body, like(k + TABLE, half, dtype=jnp.int16), (n_keep, n_got))
    n_far = over_term(n_sum, term_bits - 1)
    g_mine = call(round_add_body, like(pk, k, dtype=BF16), (g_sum, g_far))
    g_other = over_term(g_mine, 0)
    h_own = call(new_h_body, like(k, half, dtype=BF16), (n_sum, n_far, g_mine, g_other, h_old))
    h_other = over_term(h_own, 0)

    part = call(first_w_body, like(terms, k), (masked_own, h_own), flops=flops, moved=moved)
    size = terms // 4
    payload = lambda rows: like(rows + TABLE, k, dtype=jnp.int16)
    costs = dict(flops=flops // 4, moved=moved // 4)
    got = {}
    for away in (3, 2, 1):
        body = functools.partial(send_body, away=away)
        sent = call(body, payload(size), (masked_other, part, h_other), **costs)
        got[away] = over_doc(sent, away)
    body = functools.partial(gram_h_body, side_bit=term_bits - 1)
    gram = call(body, like(pk // 2, k), (h_other, h_own), **costs)
    keep = call(keep_rows_body, like(size, k), (masked_other, part, h_other), **costs)
    new_h = call(new_h_out_body, like(k, docs, dtype=BF16), (h_other, h_own))
    args = (keep, got[1], got[2], got[3])
    for bit in range(2, bits):
        last = bit == bits - 1
        rows = size if last else size // 2
        outs = (payload(rows),) if last else (payload(rows), like(rows, k))
        sent, *kept = call(functools.partial(next_step_body, bit=bit, last=last), outs, args)
        arrived = over_doc(sent, 1 << bit)
        size, args = rows, (*kept, arrived)
    share = call(total_body, like(1, size + TABLE, k, dtype=jnp.int16), (sent, arrived))
    for bit in reversed(range(2, bits - 1)):
        share = join(doc_bit(bit), share, over_doc(share, 1 << bit))
    shares = {}
    for away in (3, 1, 2):
        shares[away] = over_doc(share, away)

    for bit in range(2, bits):
        gram_got = over_doc(gram, 1 << bit)
        gram = call(add_body, like(pk // 2, k), (gram, gram_got))
    grams = {}
    for away in (3, 1, 2):
        grams[away] = over_doc(gram, away)
    g_half = call(gram_quad_body, like(pk // 2, k, dtype=BF16), (gram, grams[1], grams[2], grams[3]))
    far = term_bits - 1
    g_far = over_term(g_half, far)
    g_across = swap(g_half, "term", n_term, 1 | (1 << far))
    g_near = over_term(g_half, 0)
    body = functools.partial(ratio_body, side_bit=far)
    ratio = call(body, like(terms, k), (g_half, g_near, g_far, g_across, w), flops=flops // 4)
    new_w = call(
        new_w_body,
        like(terms, k, dtype=BF16),
        (ratio, share, shares[1], shares[2], shares[3]),
        spec=HBM,
        scratch=(pltpu.VMEM((terms, k), BF16), pltpu.SemaphoreType.DMA((4,))),
    )
    return new_w, new_h


def solution(mesh):
    sizes = dict(mesh.shape)
    return jax.shard_map(
        functools.partial(on_device, n_doc=sizes["doc"], n_term=sizes["term"]),
        mesh=mesh,
        in_specs=(P("term", "doc"), P("term", "doc"), P("term", None), P(None, "doc")),
        out_specs=(P("term", None), P(None, "doc")),
        check_vma=False,
    )
```

```python
import functools

import jax
import jax.numpy as jnp
from jax import lax
from jax.experimental import pallas as pl
from jax.experimental.pallas import tpu as pltpu
from jax.sharding import PartitionSpec as P


BLOCK = 128
F32 = jnp.float32
BF16 = jnp.bfloat16
VMEM = pl.BlockSpec(memory_space=pltpu.VMEM)
HBM = pl.BlockSpec(memory_space=pltpu.HBM)
PIECES = 1
TABLE = 8


def nt(a, b):
    return lax.dot_general(a, b, (((1,), (1,)), ((), ())), preferred_element_type=F32)


def nn(a, b):
    return lax.dot_general(a, b, (((1,), (0,)), ((), ())), preferred_element_type=F32)


def call(body, out, args, spec=None, scratch=(), flops=1 << 20, moved=1 << 20, limit=24 << 20):
    return pl.pallas_call(
        body,
        out_shape=out,
        in_specs=[VMEM] * len(args),
        out_specs=jax.tree.map(lambda _: spec or VMEM, out),
        scratch_shapes=list(scratch),
        compiler_params=pltpu.CompilerParams(vmem_limit_bytes=limit),
        cost_estimate=pl.CostEstimate(flops=flops, bytes_accessed=moved, transcendentals=0),
    )(*args)


def like(*shape, dtype=F32):
    return jax.ShapeDtypeStruct(shape, dtype)


LEVELS = 65534
PER_OCTAVE = 512
EMPTY = -32768


def limits(low, high):
    empty = high == EMPTY
    least = jnp.where(empty, 0.0, jnp.exp2(low * (1.0 / PER_OCTAVE)))
    step = jnp.where(empty, 0.0, (jnp.exp2(high * (1.0 / PER_OCTAVE)) - least) * (1.0 / LEVELS))
    return least, step


def encode(x):
    x = x * lax.rsqrt(jnp.maximum(x, 1e-30))
    least = jnp.min(x, axis=0, keepdims=True)
    most = jnp.max(x, axis=0, keepdims=True)
    octave = lambda v: jnp.log2(jnp.maximum(v, 1e-18)) * PER_OCTAVE
    empty = most <= 0.0
    low = jnp.where(empty, EMPTY, jnp.floor(octave(least) - 0.5)).astype(F32)
    high = jnp.where(empty, EMPTY, jnp.ceil(octave(most) + 0.5)).astype(F32)
    base, step = limits(low, high)
    scale = jnp.where(empty, 0.0, 1.0 / jnp.where(empty, 1.0, step))
    code = jnp.clip((x - base) * scale + 0.5, 0.0, LEVELS).astype(jnp.int32) - LEVELS // 2
    return code, low, high


def decode(code, low, high):
    base, step = limits(low, high)
    root = base + (code.astype(jnp.int32) + LEVELS // 2).astype(F32) * step
    return root * root


def put_codes(ref, first, groups):
    table = []
    for x in groups:
        code, low, high = encode(x)
        ref[first : first + x.shape[0], :] = code.astype(jnp.int16)
        table += [low, high]
        first += x.shape[0]
    return table


def put_table(ref, at, table):
    row = lax.broadcasted_iota(jnp.int32, (TABLE, table[0].shape[1]), 0)
    out = jnp.zeros(row.shape, F32)
    for i, line in enumerate(table):
        out = jnp.where(row == i, line, out)
    ref[at : at + TABLE, :] = out.astype(jnp.int32).astype(jnp.int16)


def get_table(ref, at):
    return ref[at : at + TABLE, :].astype(jnp.int32).astype(F32)


def get_codes(ref, first, rows, group, table, entry):
    out = []
    for i in range(rows // group):
        low, high = table[entry : entry + 1, :], table[entry + 1 : entry + 2, :]
        out.append(decode(ref[first + i * group : first + (i + 1) * group, :], low, high))
        entry += 2
    return jnp.concatenate(out, axis=0)


def put_parts(ref, parts):
    groups = []
    for x in parts:
        group = min(BLOCK, x.shape[0])
        groups += [x[i : i + group] for i in range(0, x.shape[0], group)]
    table = put_codes(ref, 0, groups)
    put_table(ref, sum(x.shape[0] for x in parts), table)


def get_parts(ref, sizes):
    table = get_table(ref, sum(sizes))
    out, first, entry = [], 0, 0
    for rows in sizes:
        group = min(BLOCK, rows)
        out.append(get_codes(ref, first, rows, group, table, entry))
        first += rows
        entry += 2 * (rows // group)
    return out


def core_index():
    term = lax.axis_index("term")
    return (term ^ (term >> (lax.axis_size("term").bit_length() - 2))) & 1


def term_bit(bit):
    return (lax.axis_index("term") >> bit) & 1


def quad_index():
    return lax.axis_index("doc") & 3


def doc_bit(bit):
    return (lax.axis_index("doc") >> bit) & 1


def pack(gram, core):
    k = gram.shape[0]
    h, q = k // 2, k // 4
    e = q // 2
    if core == 0:
        diag, off = gram[:h, :h], gram[:q, h:]
    else:
        diag, off = gram[h:, h:], gram[q:h, h:]
    top = jnp.concatenate([diag[:q], diag[q:]], axis=1)
    low = jnp.concatenate([off[:e], off[e:]], axis=1)
    return jnp.concatenate([top, low], axis=0)


def unpack(one, two):
    k = one.shape[1]
    h, q = k // 2, k // 4
    e = q // 2

    def parts(p):
        diag = jnp.concatenate([p[:q, :h], p[:q, h:]], axis=0)
        off = jnp.concatenate([p[q : q + e, :h], p[q : q + e, h:]], axis=0)
        return diag, off

    diag_one, off_one = parts(one)
    diag_two, off_two = parts(two)
    off = jnp.concatenate([off_one, off_two], axis=0)
    upper = jnp.concatenate([diag_one, off], axis=1)
    lower = jnp.concatenate([off.T, diag_two], axis=1)
    return jnp.concatenate([upper, lower], axis=0)


def pick(core, one, two):
    return jnp.where(core == 0, one, two)


def mask_rows(pattern, half, cols):
    blocks = cols // BLOCK
    lane = lax.broadcasted_iota(jnp.int32, (pattern.shape[0], cols), 1) // BLOCK
    mask = jnp.zeros((pattern.shape[0], cols), F32)
    for c in range(blocks):
        column = pick(half, pattern[:, c : c + 1], pattern[:, blocks + c : blocks + c + 1])
        mask = jnp.where(lane == c, column.astype(F32), mask)
    return mask


def masked_piece(tile_ref, mask, piece, rows):
    out = []
    for r in range(rows // BLOCK):
        first = piece * rows + r * BLOCK
        line = mask[first // BLOCK : first // BLOCK + 1, :].astype(BF16)
        out.append(tile_ref[first : first + BLOCK, :] * line)
    return jnp.concatenate(out, axis=0)


def gram_w_body(w, wt, send, keep):
    core = core_index()
    flipped = w[...].T
    wt[...] = flipped
    gram = nn(flipped, w[...])
    one, two = pack(gram, 0), pack(gram, 1)
    send[...] = pick(core, two, one)
    keep[...] = pick(core, one, two)


def half_h_body(h, out):
    cols = out.shape[1]
    out[...] = h[:, pl.ds(pl.multiple_of(core_index() * cols, cols), cols)]


def numer_body(m, pattern, wt, *refs, other):
    out, masked = refs[-2:]
    side = 1 - core_index() if other else core_index()
    terms, cols = masked.shape
    rows = terms // PIECES
    half = m.at[:, pl.ds(pl.multiple_of(side * cols, cols), cols)]
    mask = mask_rows(pattern[...], side, cols)
    for i in range(PIECES):
        part = slice(i * rows, (i + 1) * rows)
        tile = masked_piece(half, mask, i, rows)
        masked[part, :] = tile
        product = nn(wt[:, part], tile)
        if i == 0:
            out[...] = product
        else:
            out[...] += product


def add_body(a, b, out):
    out[...] = a[...] + b[...]


def round_add_body(a, b, out):
    out[...] = (a[...] + b[...]).astype(BF16)


def code_sum_body(a, b, out):
    total = a[...] + b[...]
    put_table(out, total.shape[0], put_codes(out, 0, [total]))


def new_h_body(mine, other, gram_mine, gram_other, h, out):
    core = core_index()
    a, b = gram_mine[...], gram_other[...]
    gram = unpack(pick(core, a, b), pick(core, b, a))
    old = h[...]
    rows = h.shape[0]
    total = None
    for ref in (mine, other):
        part = get_codes(ref, 0, rows, rows, get_table(ref, rows), 0)
        total = part if total is None else total + part
    out[...] = (old.astype(F32) * total / nn(gram, old)).astype(BF16)


def first_w_body(masked, h, out):
    step = masked.shape[0] // 2
    for r in range(2):
        part = slice(r * step, (r + 1) * step)
        out[part, :] = nt(masked[part, :], h[...])


def piece_of(masked, part, h, index, size):
    start = pl.multiple_of(index * size, size)
    return part[pl.ds(start, size), :] + nt(masked[pl.ds(start, size), :], h[...])


def send_body(masked, part, h, out, *, away):
    put_parts(out, [piece_of(masked, part, h, quad_index() ^ away, masked.shape[0] // 4)])


def keep_rows_body(masked, part, h, out):
    out[...] = piece_of(masked, part, h, quad_index(), out.shape[0])


def gram_h_body(h, h_own, out, *, side_bit):
    gram = nt(h[...], h[...]) + nt(h_own[...], h_own[...])
    part = pick(core_index(), pack(gram, 0), pack(gram, 1))
    rows = out.shape[0]
    out[...] = pick(term_bit(side_bit), part[:rows], part[rows:])


def gram_quad_body(own, one, two, three, out):
    out[...] = ((own[...] + one[...]) + (two[...] + three[...])).astype(BF16)


def new_h_out_body(h, h_own, out):
    core, cols = core_index(), h.shape[1]
    out[:, pl.ds(pl.multiple_of((1 - core) * cols, cols), cols)] = h[...]
    out[:, pl.ds(pl.multiple_of(core * cols, cols), cols)] = h_own[...]


def next_step_body(keep, *refs, bit, last):
    size = keep.shape[0]
    outs = refs[-1:] if last else refs[-2:]
    got = [get_parts(ref, (size,))[0] for ref in refs[: len(refs) - len(outs)]]
    rows = keep[...] + got[0]
    if len(got) > 1:
        rows += got[1] + got[2]
    if last:
        put_parts(outs[0], [rows])
        return
    half = size // 2
    low, high = rows[:half], rows[half:]
    side = doc_bit(bit)
    put_parts(outs[0], [pick(side, high, low)])
    outs[1][...] = pick(side, low, high)


def total_body(sent, got, out):
    size = sent.shape[0] - TABLE
    put_parts(out.at[0], [get_parts(sent, (size,))[0] + get_parts(got, (size,))[0]])


def ratio_body(here, near, far, across, w, out, *, side_bit):
    core, side = core_index(), term_bit(side_bit)

    def both(one, two):
        return jnp.concatenate([pick(side, one, two), pick(side, two, one)], axis=0)

    mine, other = both(here[...], far[...]), both(near[...], across[...])
    gram = unpack(pick(core, mine, other), pick(core, other, mine))
    old = w[...]
    out[...] = old.astype(F32) / nn(old, gram)


def new_w_body(ratio, own, one, two, three, out, held, sems):
    pieces, size = own.shape[0], own.shape[1] - TABLE
    copies = []
    for away, ref in enumerate((own, one, two, three)):
        first = (quad_index() ^ away) * pieces
        for i in range(pieces):
            rows = pl.ds(pl.multiple_of((first + i) * size, size), size)
            held[rows, :] = (ratio[rows, :] * get_parts(ref.at[i], (size,))[0]).astype(BF16)
        rows = pl.ds(pl.multiple_of(first * size, pieces * size), pieces * size)
        copies.append(pltpu.make_async_copy(held.at[rows, :], out.at[rows, :], sems.at[away]))
        copies[-1].start()
    for copy in copies:
        copy.wait()


def swap(x, axis, size, away):
    return lax.ppermute(x, axis, [(i, i ^ away) for i in range(size)])


def join(bit, mine, other):
    return jnp.concatenate([jnp.where(bit == 0, mine, other), jnp.where(bit == 0, other, mine)], axis=0)


def on_device(m, pattern, w, h, *, n_doc, n_term):
    return update(m, pattern, w, h, n_doc, n_term)


def update(m, pattern, w, h, n_doc, n_term):
    terms, docs = m.shape
    k = w.shape[1]
    half = docs // 2
    pk = 3 * k // 8
    bits = n_doc.bit_length() - 1
    term_bits = n_term.bit_length() - 1

    def over_term(x, bit):
        return swap(x, "term", n_term, 1 << bit)

    def over_doc(x, away):
        return swap(x, "doc", n_doc, away)

    flops = terms * docs * k
    moved = 2 * terms * docs

    side = like(terms, half, dtype=BF16)
    wt, g_send, g_keep = call(
        gram_w_body, (like(k, terms, dtype=BF16), like(pk, k), like(pk, k)), (w,), flops=32 * flops, moved=moved
    )
    g_got = over_term(g_send, 0)

    def numer(is_other, *after):
        body = functools.partial(numer_body, other=is_other)
        return call(body, (like(k, half), side), (m, pattern, wt, *after), flops=flops, moved=moved)

    n_send, masked_other = numer(True)
    n_got = over_term(n_send, 0)
    for bit in range(1, term_bits - 1):
        g_keep = call(add_body, like(pk, k), (g_keep, g_got))
        g_got = over_term(g_keep, bit)
    g_sum = call(add_body, like(pk, k), (g_keep, g_got))
    g_far = swap(g_sum, "term", n_term, 1 | (1 << (term_bits - 1)))
    n_keep, masked_own = numer(False, g_sum)
    h_old = call(half_h_body, like(k, half, dtype=BF16), (h,))
    for bit in range(1, term_bits - 1):
        n_keep = call(add_body, like(k, half), (n_keep, n_got))
        n_got = over_term(n_keep, bit)
    n_sum = call(code_sum_body, like(k + TABLE, half, dtype=jnp.int16), (n_keep, n_got))
    n_far = swap(n_sum, "term", n_term, 1 | (1 << (term_bits - 1)))
    g_mine = call(round_add_body, like(pk, k, dtype=BF16), (g_sum, g_far))
    g_other = over_term(g_mine, 0)
    h_own = call(new_h_body, like(k, half, dtype=BF16), (n_sum, n_far, g_mine, g_other, h_old))
    h_other = over_term(h_own, 0)

    part = call(first_w_body, like(terms, k), (masked_own, h_own), flops=flops, moved=moved)
    size = terms // 4
    payload = lambda rows: like(rows + TABLE, k, dtype=jnp.int16)
    costs = dict(flops=flops // 4, moved=moved // 4)
    got = {}
    for away in (3, 2, 1):
        body = functools.partial(send_body, away=away)
        sent = call(body, payload(size), (masked_other, part, h_other), **costs)
        got[away] = over_doc(sent, away)
    body = functools.partial(gram_h_body, side_bit=term_bits - 1)
    gram = call(body, like(pk // 2, k), (h_other, h_own), **costs)
    keep = call(keep_rows_body, like(size, k), (masked_other, part, h_other), **costs)
    new_h = call(new_h_out_body, like(k, docs, dtype=BF16), (h_other, h_own))
    args = (keep, got[1], got[2], got[3])
    for bit in range(2, bits):
        last = bit == bits - 1
        rows = size if last else size // 2
        outs = (payload(rows),) if last else (payload(rows), like(rows, k))
        sent, *kept = call(functools.partial(next_step_body, bit=bit, last=last), outs, args)
        arrived = over_doc(sent, 1 << bit)
        size, args = rows, (*kept, arrived)
    share = call(total_body, like(1, size + TABLE, k, dtype=jnp.int16), (sent, arrived))
    for bit in reversed(range(2, bits - 1)):
        share = join(doc_bit(bit), share, over_doc(share, 1 << bit))
    shares = {}
    for away in (3, 1, 2):
        shares[away] = over_doc(share, away)

    for bit in range(2, bits):
        gram_got = over_doc(gram, 1 << bit)
        gram = call(add_body, like(pk // 2, k), (gram, gram_got))
    grams = {}
    for away in (3, 1, 2):
        grams[away] = over_doc(gram, away)
    g_half = call(gram_quad_body, like(pk // 2, k, dtype=BF16), (gram, grams[1], grams[2], grams[3]))
    far = term_bits - 1
    g_far = swap(g_half, "term", n_term, 1 | (1 << far))
    g_across = over_term(g_half, far)
    g_near = over_term(g_half, 0)
    body = functools.partial(ratio_body, side_bit=far)
    ratio = call(body, like(terms, k), (g_half, g_near, g_far, g_across, w), flops=flops // 4)
    new_w = call(
        new_w_body,
        like(terms, k, dtype=BF16),
        (ratio, share, shares[1], shares[2], shares[3]),
        spec=HBM,
        scratch=(pltpu.VMEM((terms, k), BF16), pltpu.SemaphoreType.DMA((4,))),
    )
    return new_w, new_h


def solution(mesh):
    sizes = dict(mesh.shape)
    return jax.shard_map(
        functools.partial(on_device, n_doc=sizes["doc"], n_term=sizes["term"]),
        mesh=mesh,
        in_specs=(P("term", "doc"), P("term", "doc"), P("term", None), P(None, "doc")),
        out_specs=(P("term", None), P(None, "doc")),
        check_vma=False,
    )
```
